32 devices in a mesh: users: 2 (over x), hist: 8 (over z, y), head: 2 (over core).
Axes of the slice: x: 2, y: 2, z: 4, core: 2. Of those that a mesh axis runs over, the one named last changes fastest.
Arguments:
- candidates: bfloat16 [2048, 512], P(('users', 'hist')), parts along dimension 0, may hold values from -6 to 6
- key_cache: bfloat16 [2, 32768, 512], P(None, ('users', 'hist'), 'head'), parts along dimension 1, may hold values from -6 to 6
- value_cache: bfloat16 [2, 32768, 512], P(None, ('users', 'hist'), 'head'), parts along dimension 1, may hold values from -6 to 6
- w_in: bfloat16 [2, 512, 4, 512], P(None, None, None, 'head'), may hold values from -0.25 to 0.25
- w_out: bfloat16 [2, 512, 512], P(None, 'head'), may hold values from -0.25 to 0.25
- rab_table: float32 [2, 32, 8], P(None, None, 'head'), may hold values from -4 to 4
- hist_len: int32 [16], P(('users', 'hist')), parts along dimension 0, may hold values from 1 to 2048, 8192 in all
- hist_bucket: int32 [32768], P(('users', 'hist')), parts along dimension 0, may hold values from 0 to 31
- visible: int32 [8, 128], P(None, ('users', 'hist')), parts along dimension 1, may hold values 0 or 1
Outputs:
- candidate_out: bfloat16 [2048, 512], P(('users', 'hist')), parts along dimension 0
The draws below stay inside these ranges and needn't reach their ends.
There are 2 independent parts, one for each index of `users`. The reference program is written for one: setup_inputs(seed, part) draws one part's arguments, and reference() takes and returns one part's arrays. A program takes and returns all parts, laid end to end along the dimension named above; an argument that names none is the same for every part. Nothing has to cross between parts.
Inputs may be any that keep to these rules, and one draw needn't show every extreme that they name: `hist_len`: entry s counts the valid events at the start of history shard s; the entries sum to 8192 and the largest is 2048. visible[m, b] is 1 where microbatch m sees history events b * 256 to (b + 1) * 256 - 1.
All inputs are finite; a program needn't handle non-finite values.
Results may differ from the reference program's by a relative error of at most 0.019.
Values may be sent and summed in bfloat16 or wider, within the bound.
No kernel may reach another device: no remote copies, remote signals or barrier semaphores. Data moves between devices by JAX's collectives and lax.ppermute only.
A program may use at most 64 MiB of HBM per device.

```python
import math
import jax
import jax.numpy as jnp
import numpy as np
from jax import lax

D = 512
HEADS = 8
DH = 64
LAYERS = 2
NB = 32
BLOCK = 256
MICRO = 8
C = 1024
HIST_DEV = 2048
HIST = 16384
N_HIST = 8


def plant(array, rng, least, high):
    spot = [jax.random.randint(jax.random.fold_in(rng, axis), (), 0, length) for axis, length in enumerate(array.shape)]
    widest = array.shape.index(max(array.shape))
    next_to = spot[:widest] + [(spot[widest] + 1) % array.shape[widest]] + spot[widest + 1:]
    return array.at[tuple(spot)].set(least).at[tuple(next_to)].set(high)


def steps_of(rng, extent, split, low, top_value):
    loudness, own = 1.0, jax.random.fold_in(rng, 6)
    for position, parts in split:
        steps = jnp.exp(jax.random.uniform(jax.random.fold_in(own, position), (parts,), jnp.float32, low / len(split), top_value / len(split)))
        loudness = loudness * jnp.repeat(steps, extent[position] // parts).reshape([-1 if axis == position else 1 for axis in range(len(extent))])
    return loudness


def length_profile(amount, total, bound, lean):
    portions = [(1 << 20) // math.isqrt(grade ** lean) + 1 for grade in range(2, amount + 1)]
    spare, given = total - bound - (amount - 1), [1] * (amount - 1)
    while spare > 0:
        free = [i for i in range(amount - 1) if given[i] < bound]
        pool, budget = sum([portions[i] for i in free]), spare
        for i in free:
            extra = min(bound - given[i], max(1, budget * portions[i] // pool), spare)
            given[i] = given[i] + extra
            spare = spare - extra
    return np.array([bound] + given)


def uneven(own_key, amount, total, bound, lean):
    if amount == 2:
        one = jax.random.randint(own_key, (), max(1, total - bound), min(bound, total - 1) + 1)
        return jnp.stack([one, total - one])
    sizes = jnp.asarray(length_profile(amount, total, bound, lean), jnp.int32)
    twos = (amount - 1) // 2
    source_of, sink = sizes[1:1 + 2 * twos:2], sizes[2:2 + 2 * twos:2]
    slack = jnp.minimum(source_of - 1, bound - sink)
    shifted = jax.random.randint(jax.random.fold_in(own_key, 1), (twos,), 0, 1 << 20) % (slack + 1)
    sizes = sizes.at[1:1 + 2 * twos:2].set(source_of - shifted).at[2:2 + 2 * twos:2].set(sink + shifted)
    return sizes[jax.random.permutation(jax.random.fold_in(own_key, 2), amount)]


def bell_draw(rng, dims, deviation, reach, cuts=(), kind=jnp.bfloat16):
    result = deviation * jax.random.normal(rng, dims, jnp.float32)
    if cuts:
        result = result * steps_of(rng, dims, cuts, -0.22, 0.18)
    return jnp.clip(result, -reach, reach).astype(kind)


def setup_inputs(seed: int = 0, part: int = 0) -> dict:
    key_of = jax.random.split(jax.random.key(seed), 10)
    part_keys = jax.random.split(jax.random.fold_in(key_of[9], part), 10)
    candidates = bell_draw(part_keys[0], (C, D), 1.0, 6.0, ((0, 8),))
    key_cache = bell_draw(part_keys[1], (LAYERS, HIST, HEADS * DH), 1.0, 6.0, ((1, 8), (2, 2)))
    value_cache = bell_draw(part_keys[2], (LAYERS, HIST, HEADS * DH), 1.0, 6.0, ((1, 8), (2, 2)))
    w_in = bell_draw(key_of[3], (LAYERS, D, 4, HEADS * DH), D ** -0.5, 0.25, ((3, 2),))
    w_out = bell_draw(key_of[4], (LAYERS, HEADS * DH, D), (HEADS * DH) ** -0.5, 0.25, ((1, 2),))
    rab_table = bell_draw(key_of[5], (LAYERS, NB, HEADS), 1.0, 4.0, ((2, 2),), jnp.float32)
    hist_len = uneven(part_keys[6], N_HIST, N_HIST * HIST_DEV // 2, HIST_DEV, 2).astype(jnp.int32)
    hist_bucket = plant(jax.random.randint(part_keys[7], (HIST,), 0, NB), jax.random.fold_in(part_keys[7], 1), 0, NB - 1).astype(jnp.int32)
    visible = plant((jax.random.randint(part_keys[8], (MICRO, HIST // BLOCK), 0, 4) < 3).astype(jnp.int32), jax.random.fold_in(part_keys[8], 1), 0, 1)
    return dict(candidates=candidates, key_cache=key_cache, value_cache=value_cache, w_in=w_in, w_out=w_out, rab_table=rab_table, hist_len=hist_len, hist_bucket=hist_bucket, visible=visible)


epsilon = 1e-05

def reference(candidates, key_cache, value_cache, w_in, w_out, rab_table, hist_len, hist_bucket, visible):
    width = HEADS * DH
    factor = DH ** (-0.5)
    stream = candidates.astype(jnp.float32)
    micro_ids = jnp.arange(C, dtype=jnp.int32) // (C // MICRO)
    blocks_shard = HIST_DEV // BLOCK
    for layer_index in range(LAYERS):
        average = lax.optimization_barrier(jnp.mean(stream, axis=-1, keepdims=True))
        centred = stream - average
        variance = lax.optimization_barrier(jnp.mean(centred * centred, axis=-1, keepdims=True))
        normed = (centred * lax.rsqrt(variance + epsilon)).astype(jnp.bfloat16)
        projected = jnp.dot(normed, w_in[layer_index].reshape(D, 4 * width), preferred_element_type=jnp.float32)
        projected = jax.nn.silu(projected).astype(jnp.bfloat16).reshape(C, 4, width)
        queries = projected[:, 0].astype(jnp.float32).reshape(C, HEADS, DH)
        keys_new = projected[:, 1].astype(jnp.float32).reshape(C, HEADS, DH)
        values_new = projected[:, 2].astype(jnp.float32).reshape(C, HEADS, DH)
        gates = projected[:, 3].astype(jnp.float32)
        one_hot = (hist_bucket[:, None] == jnp.arange(NB, dtype=jnp.int32)[None, :]).astype(jnp.float32)
        bias = jnp.dot(one_hot, rab_table[layer_index], precision=lax.Precision.HIGHEST)
        cached_keys = key_cache[layer_index]
        cached_values = value_cache[layer_index]

        def shard_step(summed, shard):
            key_part = lax.dynamic_slice_in_dim(cached_keys, shard * HIST_DEV, HIST_DEV, 0).astype(jnp.float32).reshape(HIST_DEV, HEADS, DH)
            value_part = lax.dynamic_slice_in_dim(cached_values, shard * HIST_DEV, HIST_DEV, 0).astype(jnp.float32).reshape(HIST_DEV, HEADS, DH)
            bias_part = lax.dynamic_slice_in_dim(bias, shard * HIST_DEV, HIST_DEV, 0)
            visible_part = lax.dynamic_slice_in_dim(visible, shard * blocks_shard, blocks_shard, 1)[micro_ids]
            valid = (jnp.arange(HIST_DEV, dtype=jnp.int32) < hist_len[shard]).astype(jnp.float32)
            masking = jnp.repeat(visible_part, BLOCK, axis=1).astype(jnp.float32) * valid[None, :]
            scores = jnp.einsum('chd,khd->hck', queries, key_part) * factor + bias_part.T[:, None, :]
            weights = (jax.nn.silu(scores) * masking[None]).astype(jnp.bfloat16)
            weights = lax.optimization_barrier(weights).astype(jnp.float32)
            partial_value = jnp.einsum('hck,khd->chd', weights, value_part).astype(jnp.bfloat16)
            partial_value = lax.optimization_barrier(partial_value).astype(jnp.float32)
            return (summed + partial_value, None)
        history, _ = lax.scan(shard_step, jnp.zeros((C, HEADS, DH), jnp.float32), jnp.arange(N_HIST, dtype=jnp.int32))
        own_score = jax.nn.silu(lax.optimization_barrier(jnp.sum(queries * keys_new, axis=-1)) * factor)
        attended = (history + own_score[..., None] * values_new).reshape(C, width)
        average = lax.optimization_barrier(jnp.sum(attended, axis=-1, keepdims=True)) / width
        squares = lax.optimization_barrier(jnp.sum(attended * attended, axis=-1, keepdims=True)) / width
        normalized = (attended - average) * lax.rsqrt(squares - average * average + epsilon)
        gated = (normalized * gates).astype(jnp.bfloat16)
        stream = stream + jnp.dot(gated, w_out[layer_index], preferred_element_type=jnp.float32)
    return stream.astype(jnp.bfloat16)
```

```python
import functools
import jax
import jax.numpy as jnp
from jax import lax
from jax.experimental import pallas as pl
from jax.experimental.pallas import tpu as pltpu
from jax.sharding import PartitionSpec as P

epsilon = 1e-05
LANES = 128
F32, BF16 = jnp.float32, jnp.bfloat16
NT = (((1,), (1,)), ((), ()))
NN = (((1,), (0,)), ((), ()))
SMEM = pl.BlockSpec(memory_space=pltpu.SMEM)
VMEM = pl.BlockSpec(memory_space=pltpu.VMEM)


def half_silu(y):
    return y + y * jnp.tanh(y)


def norm_rows(x):
    mean = jnp.mean(x, axis=-1, keepdims=True)
    centred = x - mean
    variance = jnp.mean(centred * centred, axis=-1, keepdims=True)
    return (centred * lax.rsqrt(variance + epsilon)).astype(BF16)


def mm(a, b, dims=NN):
    return lax.dot_general(a, b, dims, preferred_element_type=F32)


def first_kernel(x_ref, w_ref, normed_ref, q_ref):
    normed = norm_rows(x_ref[...].astype(F32))
    normed_ref[...] = normed
    q_ref[...] = half_silu(0.5 * mm(normed, w_ref[...])).astype(BF16)


def rest_kernel(dh, normed_ref, q_ref, wk_ref, wv_ref, wg_ref, own_ref, gate_ref):
    normed = normed_ref[...]
    part = lambda w: half_silu(0.5 * mm(normed, w[...])).astype(BF16)
    product = q_ref[...].astype(F32) * part(wk_ref).astype(F32)
    head = lax.broadcasted_iota(jnp.int32, product.shape, 1) // dh
    score = jnp.zeros_like(product)
    for h in range(product.shape[1] // dh):
        total = jnp.sum(jnp.where(head == h, product, 0.0), axis=-1, keepdims=True)
        score = jnp.where(head == h, half_silu(total * (0.5 * dh**-0.5)), score)
    own_ref[...] = score * part(wv_ref).astype(F32)
    gate_ref[...] = part(wg_ref).astype(F32)


def index_kernel(micro, nblk, block, nb, len_ref, vis_ref, bucket_ref, oh_ref, list_ref):
    count = len_ref[0]
    for m in range(micro):

        def step(b, filled):
            list_ref[m, 1 + filled] = b
            ok = jnp.logical_and(vis_ref[m, b] != 0, b * block < count)
            return filled + jnp.where(ok, 1, 0)

        filled = lax.fori_loop(0, nblk, step, jnp.int32(0))
        list_ref[m, 0] = filled
        list_ref[m, 1 + filled] = nblk
    row = lax.broadcasted_iota(jnp.int32, (LANES, block), 0)
    for b in range(nblk):
        bucket = jnp.broadcast_to(bucket_ref[b : b + 1, :], (LANES, block))
        hit = jnp.logical_and(bucket == row % nb, row < 3 * nb)
        oh_ref[b * block : (b + 1) * block, :] = jnp.where(hit, 1.0, 0.0).T.astype(BF16)


def turn_kernel(nblk, block, len_ref, v_ref, vt_ref):
    count = len_ref[0]
    width = v_ref.shape[1]
    lane = lax.broadcasted_iota(jnp.int32, (width, block), 1)
    for b in range(nblk):
        turned = v_ref[b * block : (b + 1) * block, :].astype(F32).T
        vt_ref[b] = jnp.where(lane + b * block < count, turned, 0.0).astype(BF16)
    vt_ref[nblk] = jnp.zeros((width, block), BF16)


def attend_kernel(pieces, unit, nblk, block, nb, dh, order_ref, list_ref, rab_ref, k_ref, oh_ref, vt_ref, *rest):
    q_refs, out_refs = rest[:pieces], rest[pieces : 2 * pieces]
    w_ref, acc_ref = rest[2 * pieces :]
    heads = acc_ref.shape[1] // dh
    pair_width = 2 * dh
    per = q_refs[0].shape[0] // unit
    lane = lax.broadcasted_iota(jnp.int32, rab_ref.shape, 1)
    bias = 0.5 * rab_ref[...]
    high = bias.astype(BF16).astype(F32)
    mid = (bias - high).astype(BF16).astype(F32)
    low = bias - high - mid
    bias = jnp.where(lane < nb, high, jnp.where(lane < 2 * nb, mid, jnp.where(lane < 3 * nb, low, 0.0)))
    qlane = lax.broadcasted_iota(jnp.int32, (unit, pair_width), 1)
    for p in range(pieces):
        for u in range(per):
            slot = p * per + u
            rows = q_refs[p][u * unit : (u + 1) * unit, :].astype(F32) * (0.5 * dh**-0.5)
            for pair in range(heads // 2):
                part = rows[:, pair * pair_width : (pair + 1) * pair_width]
                for h in range(2):
                    mine = jnp.logical_and(qlane >= h * dh, qlane < (h + 1) * dh)
                    span = slice(h * unit, (h + 1) * unit)
                    w_ref[slot, pair, span, 0:pair_width] = jnp.where(mine, part, 0.0).astype(BF16)
                    head = 2 * pair + h
                    w_ref[slot, pair, span, pair_width:] = jnp.broadcast_to(
                        bias[head : head + 1, :], (unit, LANES)
                    ).astype(BF16)

    def one(slot, carry):
        m = order_ref[slot]
        acc_ref[slot] = jnp.zeros(acc_ref.shape[1:], F32)

        def two_blocks(t, inner):
            sums = [None] * heads
            for j in range(2):
                b = list_ref[m, 1 + 2 * t + j]
                start = pl.multiple_of(jnp.where(b == nblk, 0, b) * block, block)
                hot = oh_ref[pl.ds(start, block), :]
                for pair in range(heads // 2):
                    keys = k_ref[pl.ds(start, block), pair * pair_width : (pair + 1) * pair_width]
                    y = mm(jnp.concatenate([keys, hot], axis=1), w_ref[slot, pair], NT)
                    weights = half_silu(y).astype(BF16)
                    for h in range(2):
                        head = 2 * pair + h
                        values = vt_ref[b, head * dh : (head + 1) * dh, :]
                        term = mm(values, weights[:, h * unit : (h + 1) * unit])
                        sums[head] = term if j == 0 else sums[head] + term
            for head in range(heads):
                acc_ref[slot, head * dh : (head + 1) * dh, :] += sums[head]
            return inner

        lax.fori_loop(0, (list_ref[m, 0] + 1) // 2, two_blocks, 0)
        return carry

    lax.fori_loop(0, pieces * per, one, 0)
    for p in range(pieces):
        for u in range(per):
            out_refs[p][u * unit : (u + 1) * unit, :] = acc_ref[p * per + u].T.astype(BF16)


def combine_kernel(*refs):
    *parts, own_ref, gate_ref, out_ref = refs
    total = own_ref[...]
    for part in parts:
        total = total + part[...].astype(F32)
    width = total.shape[1]
    out_ref[:, :width] = total
    out_ref[:, width:] = gate_ref[...]


def finish_kernel(last, head_ref, mine_ref, other_ref, wa_ref, wb_ref, stream_ref, *rest):
    lead = head_ref[0] == 0
    width = mine_ref.shape[1] // 2
    mine, other = mine_ref[...], other_ref[...]
    first, second = jnp.where(lead, mine, other), jnp.where(lead, other, mine)
    att = [first[:, :width], second[:, :width]]
    gates = [first[:, width:], second[:, width:]]
    total = sum(jnp.sum(a, axis=-1, keepdims=True) for a in att) / (2 * width)
    square = sum(jnp.sum(a * a, axis=-1, keepdims=True) for a in att) / (2 * width)
    scale = lax.rsqrt(square - total * total + epsilon)
    gated = [((a - total) * scale * g).astype(BF16) for a, g in zip(att, gates)]
    wa, wb = wa_ref[...], wb_ref[...]
    update = mm(gated[0], jnp.where(lead, wa, wb)) + mm(gated[1], jnp.where(lead, wb, wa))
    stream = stream_ref[...].astype(F32) + update
    if last:
        (out_ref,) = rest
        out_ref[...] = stream.astype(BF16)
        return
    w_ref, out_ref, normed_ref, q_ref = rest
    out_ref[...] = stream
    normed = norm_rows(stream)
    normed_ref[...] = normed
    q_ref[...] = half_silu(0.5 * mm(normed, w_ref[...])).astype(BF16)


def struct(shape, kind):
    return jax.ShapeDtypeStruct(shape, kind)


def layer_of(index, array):
    shape = array.shape[1:]
    return pl.BlockSpec((None,) + shape, lambda i: (index,) + (0,) * len(shape))


def whole(array):
    return pl.BlockSpec(array.shape, lambda i: (0,) * len(array.shape))


def cost(flops, size):
    return pl.CostEstimate(flops=flops, bytes_accessed=size, transcendentals=0)


def shards(n, candidates, key_cache, value_cache, w_in, w_out, rab_table, hist_len, hist_bucket, visible):
    layers, hist_dev, width = key_cache.shape
    heads = rab_table.shape[2]
    nb = rab_table.shape[1]
    dh = width // heads
    micro, nblk = visible.shape
    block = hist_dev // nblk
    rows, d = candidates.shape
    unit = rows * n // micro
    me = lax.axis_index("hist")
    head = lax.axis_index("head").reshape(1)
    direct = rows % unit == 0

    oh, lists = pl.pallas_call(
        functools.partial(index_kernel, micro, nblk, block, nb),
        out_shape=(struct((hist_dev, LANES), BF16), struct((micro, nblk + 2), jnp.int32)),
        in_specs=[SMEM, SMEM, VMEM],
        out_specs=(VMEM, SMEM),
        cost_estimate=cost(10**8, 10**6),
    )(hist_len, visible, hist_bucket.reshape(nblk, block))

    def turned(layer):
        return pl.pallas_call(
            functools.partial(turn_kernel, nblk, block),
            grid=(1,),
            out_shape=struct((nblk + 1, width, block), BF16),
            in_specs=[SMEM, layer_of(layer, value_cache)],
            out_specs=pl.BlockSpec((nblk + 1, width, block), lambda i: (0, 0, 0)),
            cost_estimate=cost(10**8, 2 * 10**6),
        )(hist_len, value_cache)

    def attend(layer, pieces, order, vt):
        units = len(pieces) * pieces[0].shape[0] // unit
        rab = jnp.tile(rab_table[layer].T, (1, LANES // nb))
        return pl.pallas_call(
            functools.partial(attend_kernel, len(pieces), unit, nblk, block, nb, dh),
            grid=(1,),
            out_shape=[struct(p.shape, BF16) for p in pieces],
            in_specs=[SMEM, SMEM, whole(rab), layer_of(layer, key_cache), whole(oh), whole(vt)]
            + [whole(p) for p in pieces],
            out_specs=[whole(p) for p in pieces],
            scratch_shapes=[
                pltpu.VMEM((units, heads // 2, 2 * unit, 2 * LANES), BF16),
                pltpu.VMEM((units, width, unit), F32),
            ],
            compiler_params=pltpu.CompilerParams(vmem_limit_bytes=32 << 20),
            cost_estimate=cost(10**10, 4 * 10**6),
        )(order, lists, rab, key_cache, oh, vt, *pieces)

    def swap(x, k):
        return lax.ppermute(x, "hist", [(i, i ^ k) for i in range(n)])

    swap_heads = lambda x: lax.ppermute(x, "head", [(0, 1), (1, 0)])
    weights = [[w_in[layer, :, j] for j in range(4)] for layer in range(layers)]
    w_other = swap_heads(w_out)
    normed, q = pl.pallas_call(
        first_kernel,
        out_shape=(struct((rows, d), BF16), struct((rows, width), BF16)),
        cost_estimate=cost(10**8, 10**6),
    )(candidates, weights[0][0])
    stream = candidates
    for layer in range(layers):
        if direct:
            pieces = [q] + [swap(q, k) for k in range(1, n)]
            order = me ^ jnp.arange(n, dtype=jnp.int32)
            order = (order[:, None] * (rows // unit) + jnp.arange(rows // unit, dtype=jnp.int32)).reshape(-1)
        else:
            pieces = [lax.all_gather(q, "hist", axis=0, tiled=True)]
            order = jnp.arange(micro, dtype=jnp.int32)
        own, gates = pl.pallas_call(
            functools.partial(rest_kernel, dh),
            out_shape=(struct((rows, width), F32),) * 2,
            cost_estimate=cost(10**8, 10**6),
        )(normed, q, *weights[layer][1:])
        vt = turned(layer)
        outs = attend(layer, pieces, order, vt)
        if direct:
            parts = [outs[0]] + [swap(outs[k], k) for k in range(1, n)]
        else:
            moved = lax.all_to_all(outs[0].reshape(n, rows, width), "hist", 0, 0)
            parts = [moved[i] for i in range(n)]
        mine = pl.pallas_call(
            combine_kernel,
            out_shape=struct((rows, 2 * width), F32),
            cost_estimate=cost(10**6, 10**6),
        )(*parts, own, gates)
        other = swap_heads(mine)
        last = layer == layers - 1
        common = [whole(mine), whole(other), layer_of(layer, w_out), layer_of(layer, w_out), whole(stream)]
        if last:
            return pl.pallas_call(
                functools.partial(finish_kernel, True),
                grid=(1,),
                out_shape=struct((rows, d), BF16),
                in_specs=[SMEM] + common,
                out_specs=whole(stream),
                cost_estimate=cost(10**8, 10**6),
            )(head, mine, other, w_out, w_other, stream)
        outs = (struct((rows, d), F32), struct((rows, d), BF16), struct((rows, width), BF16))
        stream, normed, q = pl.pallas_call(
            functools.partial(finish_kernel, False),
            grid=(1,),
            out_shape=outs,
            in_specs=[SMEM] + common + [whole(weights[layer + 1][0])],
            out_specs=tuple(whole(o) for o in outs),
            cost_estimate=cost(10**8, 10**6),
        )(head, mine, other, w_out, w_other, stream, weights[layer + 1][0])


def solution(mesh):
    placed = (
        P(("users", "hist"), None),
        P(None, ("users", "hist"), "head"),
        P(None, ("users", "hist"), "head"),
        P(None, None, None, "head"),
        P(None, "head", None),
        P(None, None, "head"),
        P(("users", "hist")),
        P(("users", "hist")),
        P(None, ("users", "hist")),
    )
    return jax.shard_map(
        functools.partial(shards, mesh.shape["hist"]),
        mesh=mesh,
        in_specs=placed,
        out_specs=P(("users", "hist"), None),
        check_vma=False,
    )
```

```python
import functools
import jax
import jax.numpy as jnp
from jax import lax
from jax.experimental import pallas as pl
from jax.experimental.pallas import tpu as pltpu
from jax.sharding import PartitionSpec as P

epsilon = 1e-05
LANES = 128
F32, BF16 = jnp.float32, jnp.bfloat16
NT = (((1,), (1,)), ((), ()))
NN = (((1,), (0,)), ((), ()))
SMEM = pl.BlockSpec(memory_space=pltpu.SMEM)
VMEM = pl.BlockSpec(memory_space=pltpu.VMEM)


def half_silu(y):
    return y + y * jnp.tanh(y)


def norm_rows(x):
    mean = jnp.mean(x, axis=-1, keepdims=True)
    centred = x - mean
    variance = jnp.mean(centred * centred, axis=-1, keepdims=True)
    return (centred * lax.rsqrt(variance + epsilon)).astype(BF16)


def mm(a, b, dims=NN):
    return lax.dot_general(a, b, dims, preferred_element_type=F32)


def first_kernel(x_ref, w_ref, normed_ref, q_ref):
    normed = norm_rows(x_ref[...].astype(F32))
    normed_ref[...] = normed
    q_ref[...] = half_silu(0.5 * mm(normed, w_ref[0])).astype(BF16)


def rest_kernel(dh, normed_ref, q_ref, w_ref, own_ref, gate_ref):
    normed = normed_ref[...]
    part = lambda j: half_silu(0.5 * mm(normed, w_ref[j])).astype(BF16)
    product = q_ref[...].astype(F32) * part(1).astype(F32)
    head = lax.broadcasted_iota(jnp.int32, product.shape, 1) // dh
    score = jnp.zeros_like(product)
    for h in range(product.shape[1] // dh):
        total = jnp.sum(jnp.where(head == h, product, 0.0), axis=-1, keepdims=True)
        score = jnp.where(head == h, half_silu(total * (0.5 * dh**-0.5)), score)
    own_ref[...] = score * part(2).astype(F32)
    gate_ref[...] = part(3).astype(F32)


def index_kernel(micro, nblk, block, nb, len_ref, vis_ref, bucket_ref, oh_ref, list_ref):
    count = len_ref[0]
    for m in range(micro):

        def step(b, filled):
            list_ref[m, 1 + filled] = b
            ok = jnp.logical_and(vis_ref[m, b] != 0, b * block < count)
            return filled + jnp.where(ok, 1, 0)

        filled = lax.fori_loop(0, nblk, step, jnp.int32(0))
        list_ref[m, 0] = filled
        list_ref[m, 1 + filled] = nblk
    row = lax.broadcasted_iota(jnp.int32, (LANES, block), 0)
    for b in range(nblk):
        bucket = jnp.broadcast_to(bucket_ref[b : b + 1, :], (LANES, block))
        hit = jnp.logical_and(bucket == row % nb, row < 3 * nb)
        oh_ref[b * block : (b + 1) * block, :] = jnp.where(hit, 1.0, 0.0).T.astype(BF16)


def turn_kernel(nblk, block, len_ref, v_ref, vt_ref):
    count = len_ref[0]
    width = v_ref.shape[1]
    lane = lax.broadcasted_iota(jnp.int32, (width, block), 1)
    for b in range(nblk):
        turned = v_ref[b * block : (b + 1) * block, :].astype(F32).T
        vt_ref[b] = jnp.where(lane + b * block < count, turned, 0.0).astype(BF16)
    vt_ref[nblk] = jnp.zeros((width, block), BF16)


def attend_kernel(ks, pieces, layer, nblk, block, dh, me_ref, list_ref, rab_ref, k_ref, oh_ref, vt_ref, *rest):
    q_refs, out_refs = rest[:pieces], rest[pieces : 2 * pieces]
    w_ref, acc_ref = rest[2 * pieces :]
    units, width, unit = acc_ref.shape
    heads = width // dh
    pair_width = 2 * dh
    per = q_refs[0].shape[0] // unit
    nb = rab_ref.shape[1]
    table = 0.5 * jnp.concatenate([rab_ref[layer].T] * (LANES // nb), axis=1)
    lane = lax.broadcasted_iota(jnp.int32, table.shape, 1)
    high = table.astype(BF16).astype(F32)
    mid = (table - high).astype(BF16).astype(F32)
    low = table - high - mid
    bias = jnp.where(lane < nb, high, jnp.where(lane < 2 * nb, mid, jnp.where(lane < 3 * nb, low, 0.0)))
    qlane = lax.broadcasted_iota(jnp.int32, (unit, pair_width), 1)
    for p in range(pieces):
        for u in range(per):
            slot = p * per + u
            rows = q_refs[p][u * unit : (u + 1) * unit, :].astype(F32) * (0.5 * dh**-0.5)
            for pair in range(heads // 2):
                part = rows[:, pair * pair_width : (pair + 1) * pair_width]
                for h in range(2):
                    mine = jnp.logical_and(qlane >= h * dh, qlane < (h + 1) * dh)
                    span = slice(h * unit, (h + 1) * unit)
                    w_ref[slot, pair, span, 0:pair_width] = jnp.where(mine, part, 0.0).astype(BF16)
                    head = 2 * pair + h
                    w_ref[slot, pair, span, pair_width:] = jnp.broadcast_to(
                        bias[head : head + 1, :], (unit, LANES)
                    ).astype(BF16)

    def one(slot, carry):
        m = slot
        if ks is not None:
            share = units // len(ks)
            m = jnp.int32(0)
            for i, k in enumerate(ks):
                m = jnp.where(slot // share == i, (me_ref[0] ^ k) * share + slot % share, m)
        acc_ref[slot] = jnp.zeros(acc_ref.shape[1:], F32)

        def two_blocks(t, inner):
            sums = [None] * heads
            for j in range(2):
                b = list_ref[m, 1 + 2 * t + j]
                start = pl.multiple_of(jnp.where(b == nblk, 0, b) * block, block)
                hot = oh_ref[pl.ds(start, block), :]
                for pair in range(heads // 2):
                    keys = k_ref[pl.ds(start, block), pair * pair_width : (pair + 1) * pair_width]
                    y = mm(jnp.concatenate([keys, hot], axis=1), w_ref[slot, pair], NT)
                    weights = half_silu(y).astype(BF16)
                    for h in range(2):
                        head = 2 * pair + h
                        values = vt_ref[b, head * dh : (head + 1) * dh, :]
                        term = mm(values, weights[:, h * unit : (h + 1) * unit])
                        sums[head] = term if j == 0 else sums[head] + term
            for head in range(heads):
                acc_ref[slot, head * dh : (head + 1) * dh, :] += sums[head]
            return inner

        lax.fori_loop(0, (list_ref[m, 0] + 1) // 2, two_blocks, 0)
        return carry

    lax.fori_loop(0, units, one, 0)
    for p in range(pieces):
        for u in range(per):
            span = slice(u * unit, (u + 1) * unit)
            out_refs[p][span, :] = acc_ref[p * per + u].T.astype(BF16)


def combine_kernel(*refs):
    *parts, gate_ref, out_ref = refs
    total = sum(part[...].astype(F32) for part in parts)
    width = total.shape[1]
    out_ref[:, :width] = total
    out_ref[:, width:] = gate_ref[...]


def finish_kernel(layer, last, head_ref, mine_ref, other_ref, wa_ref, wb_ref, stream_ref, *rest):
    lead = head_ref[0] == 0
    width = mine_ref.shape[1] // 2
    mine, other = mine_ref[...], other_ref[...]
    first, second = jnp.where(lead, mine, other), jnp.where(lead, other, mine)
    att = [first[:, :width], second[:, :width]]
    gates = [first[:, width:], second[:, width:]]
    total = sum(jnp.sum(a, axis=-1, keepdims=True) for a in att) / (2 * width)
    square = sum(jnp.sum(a * a, axis=-1, keepdims=True) for a in att) / (2 * width)
    scale = lax.rsqrt(square - total * total + epsilon)
    gated = [((a - total) * scale * g).astype(BF16) for a, g in zip(att, gates)]
    wa, wb = wa_ref[layer], wb_ref[layer]
    update = mm(gated[0], jnp.where(lead, wa, wb)) + mm(gated[1], jnp.where(lead, wb, wa))
    stream = stream_ref[...].astype(F32) + update
    if last:
        (out_ref,) = rest
        out_ref[...] = stream.astype(BF16)
        return
    w_ref, out_ref, normed_ref, q_ref = rest
    out_ref[...] = stream
    normed = norm_rows(stream)
    normed_ref[...] = normed
    q_ref[...] = half_silu(0.5 * mm(normed, w_ref[0])).astype(BF16)


def join_kernel(*refs):
    *parts, out_ref = refs
    rows = parts[0].shape[0]
    for p, part in enumerate(parts):
        out_ref[p * rows : (p + 1) * rows, :] = part[...]


def add_kernel(pieces, *refs):
    outs, moved, own = refs[:pieces], refs[pieces], refs[pieces + 1]
    results = refs[pieces + 2 :]
    rows = outs[0].shape[0]
    for p in range(pieces):
        total = outs[p][...].astype(F32) + moved[p * rows : (p + 1) * rows, :].astype(F32)
        if p == 0:
            results[0][...] = total + own[...]
        else:
            results[p][...] = total.astype(BF16)


def struct(shape, kind):
    return jax.ShapeDtypeStruct(shape, kind)


def call(kernel, out_shape, *args, smem=(), smem_out=(), scratch=(), vmem=8, flops=10**7):
    outs = out_shape if isinstance(out_shape, (list, tuple)) else [out_shape]
    specs = [SMEM if i in smem_out else VMEM for i in range(len(outs))]
    size = sum(a.size * a.dtype.itemsize for a in args) + sum(o.size * o.dtype.itemsize for o in outs)
    return pl.pallas_call(
        kernel,
        out_shape=out_shape,
        in_specs=[SMEM if i in smem else VMEM for i in range(len(args))],
        out_specs=specs if isinstance(out_shape, (list, tuple)) else specs[0],
        scratch_shapes=list(scratch),
        compiler_params=pltpu.CompilerParams(vmem_limit_bytes=vmem << 20),
        cost_estimate=pl.CostEstimate(flops=flops, bytes_accessed=size, transcendentals=0),
    )(*args)


def shards(n, candidates, key_cache, value_cache, w_in, w_out, rab_table, hist_len, hist_bucket, visible):
    layers, hist_dev, width = key_cache.shape
    heads = rab_table.shape[2]
    nb = rab_table.shape[1]
    dh = width // heads
    micro, nblk = visible.shape
    block = hist_dev // nblk
    rows, d = candidates.shape
    unit = rows * n // micro
    per = rows // unit
    me = lax.axis_index("hist").reshape(1)
    head = lax.axis_index("head").reshape(1)
    direct = per > 0 and n >= 4 and n & (n - 1) == 0
    even = list(range(2, n, 2))[::-1]
    half = len(even) // 2

    def attend(layer, pieces, ks, keys, vt):
        units = sum(p.shape[0] for p in pieces) // unit
        return call(
            functools.partial(attend_kernel, ks, len(pieces), layer, nblk, block, dh),
            [struct(p.shape, BF16) for p in pieces],
            me, lists, rab_table, keys, oh, vt, *pieces,
            smem=(0, 1),
            scratch=[
                pltpu.VMEM((units, heads // 2, 2 * unit, 2 * LANES), BF16),
                pltpu.VMEM((units, width, unit), F32),
            ],
            vmem=16,
            flops=units * unit * hist_dev * width * 8,
        )

    def swap(x, k):
        return lax.ppermute(x, "hist", [(i, i ^ k) for i in range(n)])

    swap_heads = lambda x: lax.ppermute(x, "head", [(0, 1), (1, 0)])
    weights = [w_in[layer].transpose(1, 0, 2) for layer in range(layers)]
    normed, q = call(
        first_kernel,
        (struct((rows, d), BF16), struct((rows, width), BF16)),
        candidates, weights[0],
    )
    stream = candidates
    w_other = swap_heads(w_out)
    oh, lists = call(
        functools.partial(index_kernel, micro, nblk, block, nb),
        (struct((hist_dev, LANES), BF16), struct((micro, nblk + 2), jnp.int32)),
        hist_len, visible, hist_bucket.reshape(nblk, block),
        smem=(0, 1), smem_out=(1,),
    )
    for layer in range(layers):
        last = layer == layers - 1
        keys = key_cache[layer]
        vt = call(
            functools.partial(turn_kernel, nblk, block),
            struct((nblk + 1, width, block), BF16),
            hist_len, value_cache[layer],
            smem=(0,),
        )
        own, gates = call(
            functools.partial(rest_kernel, dh),
            (struct((rows, width), F32),) * 2,
            normed, q, weights[layer],
        )
        if not direct:
            moved = lax.all_gather(q, "hist", axis=0, tiled=True)
            (out,) = attend(layer, [moved], None, keys, vt)
            moved = lax.all_to_all(out.reshape(n, rows, width), "hist", 0, 0)
            parts = [moved[i] for i in range(n)] + [own]
        else:
            columns = [0] + even
            pieces = [q] + [swap(q, k) for k in even]
            moved = swap(call(join_kernel, struct((rows * len(pieces), width), BF16), *pieces), 1)
            outs = attend(layer, pieces[: half + 1], columns[: half + 1], keys, vt)
            (across,) = attend(layer, [moved], [k ^ 1 for k in columns], keys, vt)
            back = swap(across, 1)
            outs = outs + attend(layer, pieces[half + 1 :], columns[half + 1 :], keys, vt)
            outs = call(
                functools.partial(add_kernel, len(outs)),
                [struct((rows, width), F32)] + [struct((rows, width), BF16)] * len(even),
                *outs, back, own,
            )
            parts = [outs[0]] + [swap(out, k) for out, k in zip(outs[1:], even)]
        mine = call(combine_kernel, struct((rows, 2 * width), F32), *parts, gates)
        other = swap_heads(mine)
        common = [head, mine, other, w_out, w_other, stream]
        if last:
            return call(
                functools.partial(finish_kernel, layer, True), struct((rows, d), BF16), *common, smem=(0,)
            )
        outs = (struct((rows, d), F32), struct((rows, d), BF16), struct((rows, width), BF16))
        stream, normed, q = call(
            functools.partial(finish_kernel, layer, False), outs, *common, weights[layer + 1], smem=(0,)
        )


def solution(mesh):
    placed = (
        P(("users", "hist"), None),
        P(None, ("users", "hist"), "head"),
        P(None, ("users", "hist"), "head"),
        P(None, None, None, "head"),
        P(None, "head", None),
        P(None, None, "head"),
        P(("users", "hist")),
        P(("users", "hist")),
        P(None, ("users", "hist")),
    )
    return jax.shard_map(
        functools.partial(shards, mesh.shape["hist"]),
        mesh=mesh,
        in_specs=placed,
        out_specs=P(("users", "hist"), None),
        check_vma=False,
    )
```

```python
import functools
import jax
import jax.numpy as jnp
from jax import lax
from jax.experimental import pallas as pl
from jax.experimental.pallas import tpu as pltpu
from jax.sharding import PartitionSpec as P

epsilon = 1e-05
LANES = 128
GROUP = 2
F32, BF16 = jnp.float32, jnp.bfloat16
NT = (((1,), (1,)), ((), ()))
NN = (((1,), (0,)), ((), ()))
SMEM = pl.BlockSpec(memory_space=pltpu.SMEM)
VMEM = pl.BlockSpec(memory_space=pltpu.VMEM)


def half_silu(y):
    return y + y * jnp.tanh(y)


def norm_rows(x):
    mean = jnp.mean(x, axis=-1, keepdims=True)
    centred = x - mean
    variance = jnp.mean(centred * centred, axis=-1, keepdims=True)
    return (centred * lax.rsqrt(variance + epsilon)).astype(BF16)


def mm(a, b, dims=NN):
    return lax.dot_general(a, b, dims, preferred_element_type=F32)


def first_kernel(x_ref, w_ref, normed_ref, q_ref):
    layer = -1
    normed = norm_rows(x_ref[...].astype(F32))
    normed_ref[...] = normed
    q_ref[...] = half_silu(0.5 * mm(normed, w_ref[layer + 1, 0])).astype(BF16)


def rest_kernel(layer, dh, normed_ref, q_ref, w_ref, own_ref, gate_ref):
    normed = normed_ref[...]
    part = lambda j: half_silu(0.5 * mm(normed, w_ref[layer, j])).astype(BF16)
    product = q_ref[...].astype(F32) * part(1).astype(F32)
    head = lax.broadcasted_iota(jnp.int32, product.shape, 1) // dh
    score = jnp.zeros_like(product)
    for h in range(product.shape[1] // dh):
        total = jnp.sum(jnp.where(head == h, product, 0.0), axis=-1, keepdims=True)
        score = jnp.where(head == h, half_silu(total * (0.5 * dh**-0.5)), score)
    own_ref[...] = score * part(2).astype(F32)
    gate_ref[...] = part(3).astype(F32)


def index_kernel(plans, per, nblk, block, nb, me_ref, len_ref, vis_ref, bucket_ref, oh_ref, task_ref):
    count = len_ref[0]
    for p, ks in enumerate(plans):
        slot_row, first_row, second_row = 3 * p, 3 * p + 1, 3 * p + 2
        total = jnp.int32(0)
        for slot in range(len(ks) * max(per, 1)):
            m = (me_ref[0] ^ ks[slot // per]) * per + slot % per if per else slot
            filled = jnp.int32(0)
            for b in range(nblk):
                place = 1 + GROUP + total + filled // 2
                task_ref[slot_row, place] = slot
                task_ref[first_row + filled % 2, place] = b
                ok = jnp.logical_and(vis_ref[m, b] != 0, b * block < count)
                filled = filled + jnp.where(ok, 1, 0)
            task_ref[second_row, 1 + GROUP + total + filled // 2] = nblk
            total = total + (filled + 1) // 2
        task_ref[slot_row, 0] = total
        for place in [1 + g for g in range(GROUP)] + [1 + GROUP + total + g for g in range(2 * GROUP)]:
            task_ref[slot_row, place] = len(ks) * max(per, 1)
            task_ref[first_row, place] = nblk
            task_ref[second_row, place] = nblk
    row = lax.broadcasted_iota(jnp.int32, (LANES, LANES), 0)
    for r in range(bucket_ref.shape[0]):
        bucket = jnp.broadcast_to(bucket_ref[r : r + 1, :], (LANES, LANES))
        hit = jnp.logical_and(bucket == row % nb, row < 3 * nb)
        oh_ref[r * LANES : (r + 1) * LANES, :] = jnp.where(hit, 1.0, 0.0).T.astype(BF16)


def turn_kernel(layer, nblk, block, len_ref, v_ref, vt_ref):
    count = len_ref[0]
    width = v_ref.shape[2]
    lane = lax.broadcasted_iota(jnp.int32, (width, block), 1)
    for b in range(nblk):
        turned = v_ref[layer, b * block : (b + 1) * block, :].astype(F32).T
        vt_ref[b] = jnp.where(lane + b * block < count, turned, 0.0).astype(BF16)
    vt_ref[nblk] = jnp.zeros((width, block), BF16)


def attend_kernel(plan, pieces, layer, nblk, block, dh, task_ref, rab_ref, k_ref, oh_ref, vt_ref, *rest):
    q_refs, out_refs = rest[:pieces], rest[pieces : 2 * pieces]
    w_ref, acc_ref, *scratch = rest[2 * pieces :]
    units, width, unit = acc_ref.shape[0] - 1, acc_ref.shape[1], acc_ref.shape[2]
    heads = width // dh
    pair_width = 2 * dh
    per = q_refs[0].shape[0] // unit
    nb = rab_ref.shape[2]
    slot_row, first_row, second_row = 3 * plan, 3 * plan + 1, 3 * plan + 2
    table = 0.5 * jnp.concatenate([rab_ref[layer]] * (LANES // nb), axis=1)
    lane = lax.broadcasted_iota(jnp.int32, table.shape, 1)
    high = table.astype(BF16).astype(F32)
    mid = (table - high).astype(BF16).astype(F32)
    low = table - high - mid
    bias = jnp.where(lane < nb, high, jnp.where(lane < 2 * nb, mid, jnp.where(lane < 3 * nb, low, 0.0)))
    qlane = lax.broadcasted_iota(jnp.int32, (unit, pair_width), 1)
    for p in range(pieces):
        for u in range(per):
            slot = p * per + u
            rows = q_refs[p][u * unit : (u + 1) * unit, :].astype(F32) * (0.5 * dh**-0.5)
            for pair in range(heads // 2):
                part = rows[:, pair * pair_width : (pair + 1) * pair_width]
                for h in range(2):
                    mine = jnp.logical_and(qlane >= h * dh, qlane < (h + 1) * dh)
                    span = slice(h * unit, (h + 1) * unit)
                    w_ref[slot, pair, span, 0:pair_width] = jnp.where(mine, part, 0.0).astype(BF16)
                    head = 2 * pair + h
                    w_ref[slot, pair, span, pair_width:] = jnp.broadcast_to(
                        bias[head : head + 1, :], (unit, LANES)
                    ).astype(BF16)

    def score(t, score_ref, pair):
        slot = task_ref[slot_row, 1 + GROUP + t]
        span = slice(pair * pair_width, (pair + 1) * pair_width)
        keys, hot = [], []
        for row in (first_row, second_row):
            b = task_ref[row, 1 + GROUP + t]
            start = pl.multiple_of(jnp.where(b == nblk, 0, b) * block, block)
            keys.append(k_ref[layer, pl.ds(start, block), span])
            hot.append(oh_ref[pl.ds(start, block), :])
        left = jnp.concatenate([jnp.concatenate(keys, axis=0), jnp.concatenate(hot, axis=0)], axis=1)
        score_ref[pair] = mm(left, w_ref[slot, pair], NT)

    def weigh(score_ref, weight_ref, pair):
        weight_ref[pair] = half_silu(score_ref[pair]).astype(BF16)

    def gather(t, weight_ref, pair):
        first, second = task_ref[first_row, 1 + GROUP + t], task_ref[second_row, 1 + GROUP + t]
        terms = []
        for h in range(2):
            span = slice((2 * pair + h) * dh, (2 * pair + h + 1) * dh)
            values = jnp.concatenate([vt_ref[first, span, :], vt_ref[second, span, :]], axis=1)
            terms.append(mm(values, weight_ref[pair, :, h * unit : (h + 1) * unit]))
        return terms

    def add(t, terms):
        slot = task_ref[slot_row, 1 + GROUP + t]
        for head, term in enumerate(terms):
            acc_ref[slot, head * dh : (head + 1) * dh, :] += term

    for slot in range(units):
        acc_ref[slot] = jnp.zeros(acc_ref.shape[1:], F32)
    pairs = range(heads // 2)
    buffers = list(zip(scratch[:GROUP], scratch[GROUP:]))
    for x, (score_ref, _) in enumerate(buffers):
        for pair in pairs:
            score(x, score_ref, pair)

    def group(i, carry):
        now = GROUP * i
        terms = [[] for _ in buffers]
        for x, (score_ref, weight_ref) in enumerate(buffers):
            for pair in pairs:
                terms[x] += gather(now - GROUP + x, weight_ref, pair)
                weigh(score_ref, weight_ref, pair)
                score(now + GROUP + x, score_ref, pair)
        for x in range(GROUP):
            add(now - GROUP + x, terms[x])
        return carry

    trips = (task_ref[slot_row, 0] + GROUP - 1) // GROUP
    lax.fori_loop(0, trips, group, 0)
    for x, (_, weight_ref) in enumerate(buffers):
        t = GROUP * (trips - 1) + x
        add(t, [term for pair in pairs for term in gather(t, weight_ref, pair)])
    for p in range(pieces):
        for u in range(per):
            span = slice(u * unit, (u + 1) * unit)
            out_refs[p][span, :] = acc_ref[p * per + u].T.astype(BF16)


def combine_kernel(*refs):
    *parts, gate_ref, out_ref = refs
    total = sum(part[...].astype(F32) for part in parts)
    width = total.shape[1]
    out_ref[:, :width] = total
    out_ref[:, width:] = gate_ref[...]


def finish_kernel(layer, last, head_ref, mine_ref, other_ref, wa_ref, wb_ref, stream_ref, *rest):
    lead = head_ref[0] == 0
    width = mine_ref.shape[1] // 2
    mine, other = mine_ref[...], other_ref[...]
    first, second = jnp.where(lead, mine, other), jnp.where(lead, other, mine)
    att = [first[:, :width], second[:, :width]]
    gates = [first[:, width:], second[:, width:]]
    total = sum(jnp.sum(a, axis=-1, keepdims=True) for a in att) / (2 * width)
    square = sum(jnp.sum(a * a, axis=-1, keepdims=True) for a in att) / (2 * width)
    scale = lax.rsqrt(square - total * total + epsilon)
    gated = [((a - total) * scale * g).astype(BF16) for a, g in zip(att, gates)]
    wa, wb = wa_ref[layer], wb_ref[layer]
    update = mm(gated[0], jnp.where(lead, wa, wb)) + mm(gated[1], jnp.where(lead, wb, wa))
    stream = stream_ref[...].astype(F32) + update
    if last:
        (out_ref,) = rest
        out_ref[...] = stream.astype(BF16)
        return
    w_ref, out_ref, normed_ref, q_ref = rest
    out_ref[...] = stream
    normed = norm_rows(stream)
    normed_ref[...] = normed
    q_ref[...] = half_silu(0.5 * mm(normed, w_ref[layer + 1, 0])).astype(BF16)


def join_kernel(*refs):
    *parts, out_ref = refs
    rows = parts[0].shape[0]
    for p, part in enumerate(parts):
        out_ref[p * rows : (p + 1) * rows, :] = part[...]


def add_kernel(pieces, *refs):
    outs, moved, own = refs[:pieces], refs[pieces], refs[pieces + 1]
    results = refs[pieces + 2 :]
    rows = outs[0].shape[0]
    for p in range(pieces):
        total = outs[p][...].astype(F32) + moved[p * rows : (p + 1) * rows, :].astype(F32)
        if p == 0:
            results[0][...] = total + own[...]
        else:
            results[p][...] = total.astype(BF16)


def struct(shape, kind):
    return jax.ShapeDtypeStruct(shape, kind)


def call(kernel, out_shape, *args, smem=(), smem_out=(), scratch=(), vmem=8, flops=10**7):
    outs = out_shape if isinstance(out_shape, (list, tuple)) else [out_shape]
    specs = [SMEM if i in smem_out else VMEM for i in range(len(outs))]
    size = sum(a.size * a.dtype.itemsize for a in args) + sum(o.size * o.dtype.itemsize for o in outs)
    return pl.pallas_call(
        kernel,
        out_shape=out_shape,
        in_specs=[SMEM if i in smem else VMEM for i in range(len(args))],
        out_specs=specs if isinstance(out_shape, (list, tuple)) else specs[0],
        scratch_shapes=list(scratch),
        compiler_params=pltpu.CompilerParams(vmem_limit_bytes=vmem << 20),
        cost_estimate=pl.CostEstimate(flops=flops, bytes_accessed=size, transcendentals=0),
    )(*args)


def shards(n, candidates, key_cache, value_cache, w_in, w_out, rab_table, hist_len, hist_bucket, visible):
    layers, hist_dev, width = key_cache.shape
    heads = rab_table.shape[2]
    nb = rab_table.shape[1]
    dh = width // heads
    micro, nblk = visible.shape
    block = hist_dev // nblk
    rows, d = candidates.shape
    unit = rows * n // micro
    per = rows // unit
    me = lax.axis_index("hist").reshape(1)
    head = lax.axis_index("head").reshape(1)
    direct = per > 0 and n >= 4 and n & (n - 1) == 0
    even = list(range(2, n, 2))[::-1]
    half = len(even) // 2

    def attend(layer, pieces, plan, vt):
        units = sum(p.shape[0] for p in pieces) // unit
        return call(
            functools.partial(attend_kernel, plan, len(pieces), layer, nblk, block, dh),
            [struct(p.shape, BF16) for p in pieces],
            tasks, table, key_cache, oh, vt, *pieces,
            smem=(0,),
            scratch=[
                pltpu.VMEM((units + 1, heads // 2, 2 * unit, 2 * LANES), BF16),
                pltpu.VMEM((units + 1, width, unit), F32),
            ]
            + [pltpu.VMEM((heads // 2, 2 * block, 2 * unit), kind) for kind in [F32] * GROUP + [BF16] * GROUP],
            vmem=16,
            flops=units * unit * hist_dev * width * 8,
        )

    def swap(x, k):
        return lax.ppermute(x, "hist", [(i, i ^ k) for i in range(n)])

    swap_heads = lambda x: lax.ppermute(x, "head", [(0, 1), (1, 0)])
    weights = w_in.transpose(0, 2, 1, 3)
    table = rab_table.transpose(0, 2, 1)
    normed, q = call(
        first_kernel,
        (struct((rows, d), BF16), struct((rows, width), BF16)),
        candidates, weights,
    )
    stream = candidates
    w_other = swap_heads(w_out)
    if direct:
        columns = [0] + even
        plans = (columns[: half + 1], [k ^ 1 for k in columns], columns[half + 1 :])
    else:
        plans = (list(range(micro)),)
    capacity = max(len(p) for p in plans) * max(per, 1) * ((nblk + 1) // 2) + 3 * GROUP + 2
    oh, tasks = call(
        functools.partial(index_kernel, plans, per if direct else 0, nblk, block, nb),
        (struct((hist_dev, LANES), BF16), struct((3 * len(plans), capacity), jnp.int32)),
        me, hist_len, visible, hist_bucket.reshape(-1, LANES),
        smem=(0, 1, 2), smem_out=(1,),
    )
    for layer in range(layers):
        last = layer == layers - 1
        vt = call(
            functools.partial(turn_kernel, layer, nblk, block),
            struct((nblk + 1, width, block), BF16),
            hist_len, value_cache,
            smem=(0,),
        )
        own, gates = call(
            functools.partial(rest_kernel, layer, dh),
            (struct((rows, width), F32),) * 2,
            normed, q, weights,
        )
        if not direct:
            moved = lax.all_gather(q, "hist", axis=0, tiled=True)
            (out,) = attend(layer, [moved], 0, vt)
            moved = lax.all_to_all(out.reshape(n, rows, width), "hist", 0, 0)
            parts = [moved[i] for i in range(n)] + [own]
        else:
            pieces = [q] + [swap(q, k) for k in even]
            pieces, vt, oh, tasks, own, gates = lax.optimization_barrier((pieces, vt, oh, tasks, own, gates))
            moved = swap(call(join_kernel, struct((rows * len(pieces), width), BF16), *pieces), 1)
            outs = attend(layer, pieces[: half + 1], 0, vt)
            moved, outs = lax.optimization_barrier((moved, outs))
            (across,) = attend(layer, [moved], 1, vt)
            later, across = lax.optimization_barrier((pieces[half + 1 :], across))
            back = swap(across, 1)
            outs = outs + attend(layer, later, 2, vt)
            outs = call(
                functools.partial(add_kernel, len(outs)),
                [struct((rows, width), F32)] + [struct((rows, width), BF16)] * len(even),
                *outs, back, own,
            )
            parts = [outs[0]] + [swap(out, k) for out, k in zip(outs[1:], even)]
        mine = call(combine_kernel, struct((rows, 2 * width), F32), *parts, gates)
        other = swap_heads(mine)
        common = [head, mine, other, w_out, w_other, stream]
        if last:
            return call(
                functools.partial(finish_kernel, layer, True), struct((rows, d), BF16), *common, smem=(0,)
            )
        outs = (struct((rows, d), F32), struct((rows, d), BF16), struct((rows, width), BF16))
        stream, normed, q = call(
            functools.partial(finish_kernel, layer, False), outs, *common, weights, smem=(0,)
        )


def solution(mesh):
    placed = (
        P(("users", "hist"), None),
        P(None, ("users", "hist"), "head"),
        P(None, ("users", "hist"), "head"),
        P(None, None, None, "head"),
        P(None, "head", None),
        P(None, None, "head"),
        P(("users", "hist")),
        P(("users", "hist")),
        P(None, ("users", "hist")),
    )
    return jax.shard_map(
        functools.partial(shards, mesh.shape["hist"]),
        mesh=mesh,
        in_specs=placed,
        out_specs=P(("users", "hist"), None),
        check_vma=False,
    )
```

```python
import functools
import jax
import jax.numpy as jnp
from jax import lax
from jax.experimental import pallas as pl
from jax.experimental.pallas import tpu as pltpu
from jax.sharding import PartitionSpec as P

epsilon = 1e-05
LANES = 128
GROUP = 1
F32, BF16 = jnp.float32, jnp.bfloat16
NT = (((1,), (1,)), ((), ()))
NN = (((1,), (0,)), ((), ()))
SMEM = pl.BlockSpec(memory_space=pltpu.SMEM)
VMEM = pl.BlockSpec(memory_space=pltpu.VMEM)


def half_silu(y):
    return y + y * jnp.tanh(y)


def norm_rows(x):
    mean = jnp.mean(x, axis=-1, keepdims=True)
    centred = x - mean
    variance = jnp.mean(centred * centred, axis=-1, keepdims=True)
    return (centred * lax.rsqrt(variance + epsilon)).astype(BF16)


def mm(a, b, dims=NN):
    return lax.dot_general(a, b, dims, preferred_element_type=F32)


def first_kernel(x_ref, w_ref, normed_ref, q_ref):
    layer = -1
    normed = norm_rows(x_ref[...].astype(F32))
    normed_ref[...] = normed
    q_ref[...] = half_silu(0.5 * mm(normed, w_ref[layer + 1, 0])).astype(BF16)


def rest_kernel(layer, dh, normed_ref, q_ref, w_ref, own_ref, gate_ref):
    normed = normed_ref[...]
    part = lambda j: half_silu(0.5 * mm(normed, w_ref[layer, j])).astype(BF16)
    product = q_ref[...].astype(F32) * part(1).astype(F32)
    head = lax.broadcasted_iota(jnp.int32, product.shape, 1) // dh
    score = jnp.zeros_like(product)
    for h in range(product.shape[1] // dh):
        total = jnp.sum(jnp.where(head == h, product, 0.0), axis=-1, keepdims=True)
        score = jnp.where(head == h, half_silu(total * (0.5 * dh**-0.5)), score)
    own_ref[...] = score * part(2).astype(F32)
    gate_ref[...] = part(3).astype(F32)


def index_kernel(plans, per, nblk, block, nb, len_ref, vis_ref, bucket_ref, oh_ref, task_ref):
    count = len_ref[0]
    me = lax.axis_index("hist")
    for p, ks in enumerate(plans):
        slot_row, first_row, second_row = 3 * p, 3 * p + 1, 3 * p + 2
        total = jnp.int32(0)
        for slot in range(len(ks) * max(per, 1)):
            m = (me ^ ks[slot // per]) * per + slot % per if per else slot
            filled = jnp.int32(0)
            for b in range(nblk):
                place = 1 + total + filled // 2
                task_ref[slot_row, place] = slot
                task_ref[first_row + filled % 2, place] = b
                ok = jnp.logical_and(vis_ref[m, b] != 0, b * block < count)
                filled = filled + jnp.where(ok, 1, 0)
            task_ref[second_row, 1 + total + filled // 2] = nblk
            total = total + (filled + 1) // 2
        task_ref[slot_row, 0] = total
        for place in [1 + total + g for g in range(3 * GROUP)]:
            task_ref[slot_row, place] = len(ks) * max(per, 1)
            task_ref[first_row, place] = nblk
            task_ref[second_row, place] = nblk
    row = lax.broadcasted_iota(jnp.int32, (LANES, LANES), 0)
    for r in range(bucket_ref.shape[0]):
        bucket = jnp.broadcast_to(bucket_ref[r : r + 1, :], (LANES, LANES))
        hit = jnp.logical_and(bucket == row % nb, row < 3 * nb)
        oh_ref[r * LANES : (r + 1) * LANES, :] = jnp.where(hit, 1.0, 0.0).T.astype(BF16)


def turn_kernel(layer, nblk, block, len_ref, v_ref, vt_ref):
    count = len_ref[0]
    width = v_ref.shape[2]
    lane = lax.broadcasted_iota(jnp.int32, (width, block), 1)
    for b in range(nblk):
        turned = v_ref[layer, b * block : (b + 1) * block, :].astype(F32).T
        vt_ref[b] = jnp.where(lane + b * block < count, turned, 0.0).astype(BF16)
    vt_ref[nblk] = jnp.zeros((width, block), BF16)


def attend_kernel(plan, pieces, outs, layer, nblk, block, dh, task_ref, rab_ref, k_ref, oh_ref, vt_ref, *rest):
    q_refs, out_refs = rest[:pieces], rest[pieces : pieces + outs]
    w_ref, acc_ref, *scratch = rest[pieces + outs :]
    units, width, unit = acc_ref.shape[0] - 1, acc_ref.shape[1], acc_ref.shape[2]
    heads = width // dh
    pair_width = 2 * dh
    per = q_refs[0].shape[0] // unit
    nb = rab_ref.shape[2]
    slot_row, first_row, second_row = 3 * plan, 3 * plan + 1, 3 * plan + 2
    table = 0.5 * jnp.concatenate([rab_ref[layer]] * (LANES // nb), axis=1)
    lane = lax.broadcasted_iota(jnp.int32, table.shape, 1)
    high = table.astype(BF16).astype(F32)
    mid = (table - high).astype(BF16).astype(F32)
    low = table - high - mid
    bias = jnp.where(lane < nb, high, jnp.where(lane < 2 * nb, mid, jnp.where(lane < 3 * nb, low, 0.0)))
    qlane = lax.broadcasted_iota(jnp.int32, (unit, pair_width), 1)
    for p in range(pieces):
        for u in range(per):
            slot = p * per + u
            rows = q_refs[p][u * unit : (u + 1) * unit, :].astype(F32) * (0.5 * dh**-0.5)
            for pair in range(heads // 2):
                part = rows[:, pair * pair_width : (pair + 1) * pair_width]
                for h in range(2):
                    mine = jnp.logical_and(qlane >= h * dh, qlane < (h + 1) * dh)
                    span = slice(h * unit, (h + 1) * unit)
                    w_ref[slot, pair, span, 0:pair_width] = jnp.where(mine, part, 0.0).astype(BF16)
                    head = 2 * pair + h
                    w_ref[slot, pair, span, pair_width:] = jnp.broadcast_to(
                        bias[head : head + 1, :], (unit, LANES)
                    ).astype(BF16)

    def score(t, score_ref, pair):
        slot = task_ref[slot_row, 1 + t]
        span = slice(pair * pair_width, (pair + 1) * pair_width)
        keys, hot = [], []
        for row in (first_row, second_row):
            b = task_ref[row, 1 + t]
            start = pl.multiple_of(jnp.where(b == nblk, 0, b) * block, block)
            keys.append(k_ref[layer, pl.ds(start, block), span])
            hot.append(oh_ref[pl.ds(start, block), :])
        left = jnp.concatenate([jnp.concatenate(keys, axis=0), jnp.concatenate(hot, axis=0)], axis=1)
        score_ref[pair] = mm(left, w_ref[slot, pair], NT)

    def gather(t, score_ref, pair):
        first, second = task_ref[first_row, 1 + t], task_ref[second_row, 1 + t]
        weights = half_silu(score_ref[pair]).astype(BF16)
        terms = []
        for h in range(2):
            span = slice((2 * pair + h) * dh, (2 * pair + h + 1) * dh)
            values = jnp.concatenate([vt_ref[first, span, :], vt_ref[second, span, :]], axis=1)
            terms.append(mm(values, weights[:, h * unit : (h + 1) * unit]))
        return terms

    def add(t, terms):
        slot = task_ref[slot_row, 1 + t]
        for head, term in enumerate(terms):
            acc_ref[slot, head * dh : (head + 1) * dh, :] += term

    for slot in range(units):
        acc_ref[slot] = jnp.zeros(acc_ref.shape[1:], F32)
    pairs = range(heads // 2)
    sets = (scratch[:GROUP], scratch[GROUP:])
    for x in range(GROUP):
        for pair in pairs:
            score(x, sets[0][x], pair)

    def group(i, carry):
        for side in range(2):
            now = GROUP * (2 * i + side)
            terms = [[] for _ in range(GROUP)]
            for x in range(GROUP):
                for pair in pairs:
                    score(now + GROUP + x, sets[1 - side][x], pair)
                    terms[x] += gather(now + x, sets[side][x], pair)
            for x in range(GROUP):
                add(now + x, terms[x])
        return carry

    lax.fori_loop(0, (task_ref[slot_row, 0] + 2 * GROUP - 1) // (2 * GROUP), group, 0)
    share = units // outs
    for slot in range(units):
        place = slot % share * unit
        out_refs[slot // share][place : place + unit, :] = acc_ref[slot].T.astype(BF16)


def combine_kernel(*refs):
    *parts, gate_ref, out_ref = refs
    total = sum(part[...].astype(F32) for part in parts)
    width = total.shape[1]
    out_ref[:, :width] = total
    out_ref[:, width:] = gate_ref[...]


def finish_kernel(layer, last, mine_ref, other_ref, wa_ref, wb_ref, stream_ref, *rest):
    lead = lax.axis_index("head") == 0
    width = mine_ref.shape[1] // 2
    mine, other = mine_ref[...], other_ref[...]
    first, second = jnp.where(lead, mine, other), jnp.where(lead, other, mine)
    att = [first[:, :width], second[:, :width]]
    gates = [first[:, width:], second[:, width:]]
    total = sum(jnp.sum(a, axis=-1, keepdims=True) for a in att) / (2 * width)
    square = sum(jnp.sum(a * a, axis=-1, keepdims=True) for a in att) / (2 * width)
    scale = lax.rsqrt(square - total * total + epsilon)
    gated = [((a - total) * scale * g).astype(BF16) for a, g in zip(att, gates)]
    wa, wb = wa_ref[layer], wb_ref[layer]
    update = mm(gated[0], jnp.where(lead, wa, wb)) + mm(gated[1], jnp.where(lead, wb, wa))
    stream = stream_ref[...].astype(F32) + update
    if last:
        (out_ref,) = rest
        out_ref[...] = stream.astype(BF16)
        return
    w_ref, out_ref, normed_ref, q_ref = rest
    out_ref[...] = stream
    normed = norm_rows(stream)
    normed_ref[...] = normed
    q_ref[...] = half_silu(0.5 * mm(normed, w_ref[layer + 1, 0])).astype(BF16)


def add_kernel(owns, pieces, *refs):
    outs, moved = refs[:pieces], refs[pieces]
    results = refs[pieces + 1 + owns :]
    rows = outs[0].shape[0]
    for p in range(pieces):
        total = outs[p][...].astype(F32) + moved[p * rows : (p + 1) * rows, :].astype(F32)
        if owns and p == pieces - 1:
            results[p][...] = total + refs[pieces + 1][...]
        else:
            results[p][...] = total.astype(BF16)


def struct(shape, kind):
    return jax.ShapeDtypeStruct(shape, kind)


def call(kernel, out_shape, *args, smem=(), smem_out=(), scratch=(), vmem=8, flops=10**7):
    outs = out_shape if isinstance(out_shape, (list, tuple)) else [out_shape]
    specs = [SMEM if i in smem_out else VMEM for i in range(len(outs))]
    size = sum(a.size * a.dtype.itemsize for a in args) + 4 * len(outs)
    return pl.pallas_call(
        kernel,
        out_shape=out_shape,
        in_specs=[SMEM if i in smem else VMEM for i in range(len(args))],
        out_specs=specs if isinstance(out_shape, (list, tuple)) else specs[0],
        scratch_shapes=list(scratch),
        compiler_params=pltpu.CompilerParams(vmem_limit_bytes=vmem << 20),
        cost_estimate=pl.CostEstimate(flops=flops, bytes_accessed=size, transcendentals=0),
    )(*args)


def shards(n, candidates, key_cache, value_cache, w_in, w_out, rab_table, hist_len, hist_bucket, visible):
    layers, hist_dev, width = key_cache.shape
    heads = rab_table.shape[2]
    nb = rab_table.shape[1]
    dh = width // heads
    micro, nblk = visible.shape
    block = hist_dev // nblk
    rows, d = candidates.shape
    unit = rows * n // micro
    per = rows // unit
    direct = per > 0 and n >= 4 and n & (n - 1) == 0
    even = list(range(2, n, 2))[::-1]

    def attend(layer, pieces, plan, vt, outs):
        units = sum(p.shape[0] for p in pieces) // unit
        return call(
            functools.partial(attend_kernel, plan, len(pieces), outs, layer, nblk, block, dh),
            [struct((units * unit // outs, width), BF16)] * outs,
            pltpu.with_memory_space_constraint(tasks, pltpu.SMEM), table, key_cache, oh, vt, *pieces,
            smem=(0,),
            scratch=[
                pltpu.VMEM((units + 1, heads // 2, 2 * unit, 2 * LANES), BF16),
                pltpu.VMEM((units + 1, width, unit), F32),
            ]
            + [pltpu.VMEM((heads // 2, 2 * block, 2 * unit), kind) for kind in [F32] * (2 * GROUP)],
            vmem=16,
            flops=units * unit * hist_dev * width * 8,
        )

    def swap(x, k):
        return lax.ppermute(x, "hist", [(i, i ^ k) for i in range(n)])

    swap_heads = lambda x: lax.ppermute(x, "head", [(0, 1), (1, 0)])
    weights = w_in.transpose(0, 2, 1, 3)
    table = rab_table.transpose(0, 2, 1)
    normed, q = call(
        first_kernel,
        (struct((rows, d), BF16), struct((rows, width), BF16)),
        candidates, weights,
    )
    stream = candidates
    w_other = swap_heads(w_out)
    if direct:
        columns = even + [0]
        half = n // 4
        first, later = [0] + even[: half - 1], even[half - 1 :]
        plans = (first, [k ^ 1 for k in columns], later)
    else:
        plans = (list(range(micro)),)
    capacity = max(len(p) for p in plans) * max(per, 1) * ((nblk + 1) // 2) + 3 * GROUP + 2
    oh, tasks = call(
        functools.partial(index_kernel, plans, per if direct else 0, nblk, block, nb),
        (struct((hist_dev, LANES), BF16), pltpu.SMEM((3 * len(plans), capacity), jnp.int32)),
        hist_len, visible, hist_bucket.reshape(-1, LANES),
        smem=(0, 1), smem_out=(1,),
    )
    for layer in range(layers):
        last = layer == layers - 1
        vt = call(
            functools.partial(turn_kernel, layer, nblk, block),
            struct((nblk + 1, width, block), BF16),
            hist_len, value_cache,
            smem=(0,),
        )
        own, gates = call(
            functools.partial(rest_kernel, layer, dh),
            (struct((rows, width), F32),) * 2,
            normed, q, weights,
        )
        if not direct:
            moved = lax.all_gather(q, "hist", axis=0, tiled=True)
            (out,) = attend(layer, [moved], 0, vt, 1)
            moved = lax.all_to_all(out.reshape(n, rows, width), "hist", 0, 0)
            parts = [moved[i] for i in range(n)] + [own]
        else:
            near = {0: q}
            for k in even:
                near[k] = swap(q, k)
            across = [swap(near[k], 1) for k in columns]
            if layer == 0:
                w_other, near[0] = lax.optimization_barrier((w_other, near[0]))
            outs = dict(zip(first, attend(layer, [near[k] for k in first], 0, vt, half)))
            across, keep = lax.optimization_barrier((across, outs[0]))
            outs[0] = keep
            far = attend(layer, across, 1, vt, 2)
            pending = [near[k] for k in later]
            far, pending = lax.optimization_barrier((far, pending))
            back = [swap(f, 1) for f in far]
            outs.update(zip(later, attend(layer, pending, 2, vt, half)))
            sums = {}
            for side, ks in enumerate((columns[:half], columns[half:])):
                kinds = [F32 if k == 0 else BF16 for k in ks]
                totals = call(
                    functools.partial(add_kernel, int(0 in ks), half),
                    [struct((rows, width), kind) for kind in kinds],
                    *[outs[k] for k in ks], back[side], *([own] if 0 in ks else []),
                )
                sums.update(zip(ks, totals))
            parts = [sums[0]] + [swap(sums[k], k) for k in even]
        mine = call(combine_kernel, struct((rows, 2 * width), F32), *parts, gates)
        other = swap_heads(mine)
        common = [mine, other, w_out, w_other, stream]
        if last:
            return call(
                functools.partial(finish_kernel, layer, True), struct((rows, d), BF16), *common
            )
        outs = (struct((rows, d), F32), struct((rows, d), BF16), struct((rows, width), BF16))
        stream, normed, q = call(
            functools.partial(finish_kernel, layer, False), outs, *common, weights
        )


def solution(mesh):
    placed = (
        P(("users", "hist"), None),
        P(None, ("users", "hist"), "head"),
        P(None, ("users", "hist"), "head"),
        P(None, None, None, "head"),
        P(None, "head", None),
        P(None, None, "head"),
        P(("users", "hist")),
        P(("users", "hist")),
        P(None, ("users", "hist")),
    )
    return jax.shard_map(
        functools.partial(shards, mesh.shape["hist"]),
        mesh=mesh,
        in_specs=placed,
        out_specs=P(("users", "hist"), None),
        check_vma=False,
    )
```

```python
import functools
import jax
import jax.numpy as jnp
from jax import lax
from jax.experimental import pallas as pl
from jax.experimental.pallas import tpu as pltpu
from jax.sharding import PartitionSpec as P

epsilon = 1e-05
LANES = 128
GROUP = 1
F32, BF16 = jnp.float32, jnp.bfloat16
NT = (((1,), (1,)), ((), ()))
NN = (((1,), (0,)), ((), ()))
SMEM = pl.BlockSpec(memory_space=pltpu.SMEM)
VMEM = pl.BlockSpec(memory_space=pltpu.VMEM)


def half_silu(y):
    return y + y * jnp.tanh(y)


def norm_rows(x):
    mean = jnp.mean(x, axis=-1, keepdims=True)
    centred = x - mean
    variance = jnp.mean(centred * centred, axis=-1, keepdims=True)
    return (centred * lax.rsqrt(variance + epsilon)).astype(BF16)


def mm(a, b, dims=NN):
    return lax.dot_general(a, b, dims, preferred_element_type=F32)


def first_kernel(x_ref, w_ref, normed_ref, q_ref):
    layer = -1
    normed = norm_rows(x_ref[...].astype(F32))
    normed_ref[...] = normed
    q_ref[...] = half_silu(0.5 * mm(normed, w_ref[layer + 1, 0])).astype(BF16)


def rest_kernel(layer, dh, normed_ref, q_ref, w_ref, own_ref, gate_ref):
    normed = normed_ref[...]
    part = lambda j: half_silu(0.5 * mm(normed, w_ref[layer, j])).astype(BF16)
    product = q_ref[...].astype(F32) * part(1).astype(F32)
    head = lax.broadcasted_iota(jnp.int32, product.shape, 1) // dh
    score = jnp.zeros_like(product)
    for h in range(product.shape[1] // dh):
        total = jnp.sum(jnp.where(head == h, product, 0.0), axis=-1, keepdims=True)
        score = jnp.where(head == h, half_silu(total * (0.5 * dh**-0.5)), score)
    own_ref[...] = score * part(2).astype(F32)
    gate_ref[...] = part(3).astype(F32)


def index_kernel(plans, per, nblk, block, nb, len_ref, vis_ref, bucket_ref, oh_ref, task_ref):
    count = len_ref[0]
    me = lax.axis_index("hist")
    for p, ks in enumerate(plans):
        slot_row, first_row, second_row = 3 * p, 3 * p + 1, 3 * p + 2
        total = jnp.int32(0)
        for slot in range(len(ks) * max(per, 1)):
            m = (me ^ ks[slot // per]) * per + slot % per if per else slot
            filled = jnp.int32(0)
            for b in range(nblk):
                place = 1 + total + filled // 2
                task_ref[slot_row, place] = slot
                task_ref[first_row + filled % 2, place] = b
                ok = jnp.logical_and(vis_ref[m, b] != 0, b * block < count)
                filled = filled + jnp.where(ok, 1, 0)
            task_ref[second_row, 1 + total + filled // 2] = nblk
            total = total + (filled + 1) // 2
        task_ref[slot_row, 0] = total
        for place in [1 + total + g for g in range(3 * GROUP)]:
            task_ref[slot_row, place] = len(ks) * max(per, 1)
            task_ref[first_row, place] = nblk
            task_ref[second_row, place] = nblk
    row = lax.broadcasted_iota(jnp.int32, (LANES, LANES), 0)
    for r in range(bucket_ref.shape[0]):
        bucket = jnp.broadcast_to(bucket_ref[r : r + 1, :], (LANES, LANES))
        hit = jnp.logical_and(bucket == row % nb, row < 3 * nb)
        oh_ref[r * LANES : (r + 1) * LANES, :] = jnp.where(hit, 1.0, 0.0).T.astype(BF16)


def turn_kernel(layer, nblk, block, len_ref, v_ref, vt_ref):
    count = len_ref[0]
    width = v_ref.shape[2]
    lane = lax.broadcasted_iota(jnp.int32, (width, block), 1)
    for b in range(nblk):
        turned = v_ref[layer, b * block : (b + 1) * block, :].astype(F32).T
        vt_ref[b] = jnp.where(lane + b * block < count, turned, 0.0).astype(BF16)
    vt_ref[nblk] = jnp.zeros((width, block), BF16)


def attend_kernel(plan, pieces, outs, layer, nblk, block, dh, task_ref, rab_ref, k_ref, oh_ref, vt_ref, *rest):
    q_refs, out_refs = rest[:pieces], rest[pieces : pieces + outs]
    w_ref, acc_ref, *scratch = rest[pieces + outs :]
    units, width, unit = acc_ref.shape[0] - 1, acc_ref.shape[1], acc_ref.shape[2]
    heads = width // dh
    pair_width = 2 * dh
    per = q_refs[0].shape[0] // unit
    nb = rab_ref.shape[2]
    slot_row, first_row, second_row = 3 * plan, 3 * plan + 1, 3 * plan + 2
    table = 0.5 * jnp.concatenate([rab_ref[layer]] * (LANES // nb), axis=1)
    lane = lax.broadcasted_iota(jnp.int32, table.shape, 1)
    high = table.astype(BF16).astype(F32)
    mid = (table - high).astype(BF16).astype(F32)
    low = table - high - mid
    bias = jnp.where(lane < nb, high, jnp.where(lane < 2 * nb, mid, jnp.where(lane < 3 * nb, low, 0.0)))
    qlane = lax.broadcasted_iota(jnp.int32, (unit, pair_width), 1)
    for p in range(pieces):
        for u in range(per):
            slot = p * per + u
            rows = q_refs[p][u * unit : (u + 1) * unit, :].astype(F32) * (0.5 * dh**-0.5)
            for pair in range(heads // 2):
                part = rows[:, pair * pair_width : (pair + 1) * pair_width]
                for h in range(2):
                    mine = jnp.logical_and(qlane >= h * dh, qlane < (h + 1) * dh)
                    span = slice(h * unit, (h + 1) * unit)
                    w_ref[slot, pair, span, 0:pair_width] = jnp.where(mine, part, 0.0).astype(BF16)
                    head = 2 * pair + h
                    w_ref[slot, pair, span, pair_width:] = jnp.broadcast_to(
                        bias[head : head + 1, :], (unit, LANES)
                    ).astype(BF16)

    def score(t, score_ref, pair):
        slot = task_ref[slot_row, 1 + t]
        span = slice(pair * pair_width, (pair + 1) * pair_width)
        keys, hot = [], []
        for row in (first_row, second_row):
            b = task_ref[row, 1 + t]
            start = pl.multiple_of(jnp.where(b == nblk, 0, b) * block, block)
            keys.append(k_ref[layer, pl.ds(start, block), span])
            hot.append(oh_ref[pl.ds(start, block), :])
        left = jnp.concatenate([jnp.concatenate(keys, axis=0), jnp.concatenate(hot, axis=0)], axis=1)
        score_ref[pair] = mm(left, w_ref[slot, pair], NT)

    def gather(t, score_ref, pair):
        first, second = task_ref[first_row, 1 + t], task_ref[second_row, 1 + t]
        weights = half_silu(score_ref[pair]).astype(BF16)
        terms = []
        for h in range(2):
            span = slice((2 * pair + h) * dh, (2 * pair + h + 1) * dh)
            values = jnp.concatenate([vt_ref[first, span, :], vt_ref[second, span, :]], axis=1)
            terms.append(mm(values, weights[:, h * unit : (h + 1) * unit]))
        return terms

    def add(t, terms):
        slot = task_ref[slot_row, 1 + t]
        for head, term in enumerate(terms):
            acc_ref[slot, head * dh : (head + 1) * dh, :] += term

    for slot in range(units):
        acc_ref[slot] = jnp.zeros(acc_ref.shape[1:], F32)
    pairs = range(heads // 2)
    sets = (scratch[:GROUP], scratch[GROUP:])
    for x in range(GROUP):
        for pair in pairs:
            score(x, sets[0][x], pair)

    def group(i, carry):
        for side in range(2):
            now = GROUP * (2 * i + side)
            terms = [[] for _ in range(GROUP)]
            for x in range(GROUP):
                for pair in pairs:
                    score(now + GROUP + x, sets[1 - side][x], pair)
                    terms[x] += gather(now + x, sets[side][x], pair)
            for x in range(GROUP):
                add(now + x, terms[x])
        return carry

    lax.fori_loop(0, (task_ref[slot_row, 0] + 2 * GROUP - 1) // (2 * GROUP), group, 0)
    share = units // outs
    for slot in range(units):
        place = slot % share * unit
        out_refs[slot // share][place : place + unit, :] = acc_ref[slot].T.astype(BF16)


def combine_kernel(*refs):
    *parts, gate_ref, out_ref = refs
    total = sum(part[...].astype(F32) for part in parts)
    width = total.shape[1]
    out_ref[:, :width] = total
    out_ref[:, width:] = gate_ref[...]


def finish_kernel(layer, last, mine_ref, other_ref, wa_ref, wb_ref, stream_ref, *rest):
    lead = lax.axis_index("head") == 0
    width = mine_ref.shape[1] // 2
    mine, other = mine_ref[...], other_ref[...]
    first, second = jnp.where(lead, mine, other), jnp.where(lead, other, mine)
    att = [first[:, :width], second[:, :width]]
    gates = [first[:, width:], second[:, width:]]
    total = sum(jnp.sum(a, axis=-1, keepdims=True) for a in att) / (2 * width)
    square = sum(jnp.sum(a * a, axis=-1, keepdims=True) for a in att) / (2 * width)
    scale = lax.rsqrt(square - total * total + epsilon)
    gated = [((a - total) * scale * g).astype(BF16) for a, g in zip(att, gates)]
    wa, wb = wa_ref[layer], wb_ref[layer]
    update = mm(gated[0], jnp.where(lead, wa, wb)) + mm(gated[1], jnp.where(lead, wb, wa))
    stream = stream_ref[...].astype(F32) + update
    if last:
        (out_ref,) = rest
        out_ref[...] = stream.astype(BF16)
        return
    w_ref, out_ref, normed_ref, q_ref = rest
    out_ref[...] = stream
    normed = norm_rows(stream)
    normed_ref[...] = normed
    q_ref[...] = half_silu(0.5 * mm(normed, w_ref[layer + 1, 0])).astype(BF16)


def add_kernel(owns, pieces, *refs):
    outs, moved = refs[:pieces], refs[pieces]
    results = refs[pieces + 1 + owns :]
    rows = outs[0].shape[0]
    for p in range(pieces):
        total = outs[p][...].astype(F32) + moved[p * rows : (p + 1) * rows, :].astype(F32)
        if owns and p == pieces - 1:
            results[p][...] = total + refs[pieces + 1][...]
        else:
            results[p][...] = total.astype(BF16)


def struct(shape, kind):
    return jax.ShapeDtypeStruct(shape, kind)


def call(kernel, out_shape, *args, smem=(), smem_out=(), scratch=(), vmem=8, flops=10**7):
    outs = out_shape if isinstance(out_shape, (list, tuple)) else [out_shape]
    specs = [SMEM if i in smem_out else VMEM for i in range(len(outs))]
    size = sum(a.size * a.dtype.itemsize for a in args) + 4 * len(outs)
    return pl.pallas_call(
        kernel,
        out_shape=out_shape,
        in_specs=[SMEM if i in smem else VMEM for i in range(len(args))],
        out_specs=specs if isinstance(out_shape, (list, tuple)) else specs[0],
        scratch_shapes=list(scratch),
        compiler_params=pltpu.CompilerParams(vmem_limit_bytes=vmem << 20),
        cost_estimate=pl.CostEstimate(flops=flops, bytes_accessed=size, transcendentals=0),
    )(*args)


def shards(n, candidates, key_cache, value_cache, w_in, w_out, rab_table, hist_len, hist_bucket, visible):
    layers, hist_dev, width = key_cache.shape
    heads = rab_table.shape[2]
    nb = rab_table.shape[1]
    dh = width // heads
    micro, nblk = visible.shape
    block = hist_dev // nblk
    rows, d = candidates.shape
    unit = rows * n // micro
    per = rows // unit
    direct = per > 0 and n >= 4 and n & (n - 1) == 0
    even = list(range(2, n, 2))[::-1]

    def attend(layer, pieces, plan, vt, outs):
        units = sum(p.shape[0] for p in pieces) // unit
        return call(
            functools.partial(attend_kernel, plan, len(pieces), outs, layer, nblk, block, dh),
            [struct((units * unit // outs, width), BF16)] * outs,
            pltpu.with_memory_space_constraint(tasks, pltpu.SMEM), table, key_cache, oh, vt, *pieces,
            smem=(0,),
            scratch=[
                pltpu.VMEM((units + 1, heads // 2, 2 * unit, 2 * LANES), BF16),
                pltpu.VMEM((units + 1, width, unit), F32),
            ]
            + [pltpu.VMEM((heads // 2, 2 * block, 2 * unit), kind) for kind in [F32] * (2 * GROUP)],
            vmem=16,
            flops=units * unit * hist_dev * width * 8,
        )

    def swap(x, k):
        return lax.ppermute(x, "hist", [(i, i ^ k) for i in range(n)])

    swap_heads = lambda x: lax.ppermute(x, "head", [(0, 1), (1, 0)])
    weights = w_in.transpose(0, 2, 1, 3)
    table = rab_table.transpose(0, 2, 1)
    normed, q = call(
        first_kernel,
        (struct((rows, d), BF16), struct((rows, width), BF16)),
        candidates, weights,
    )
    stream = candidates
    w_other = swap_heads(w_out)
    if direct:
        columns = even + [0]
        half = n // 4
        first, later = columns[:half], columns[half:]
        plans = (first, [k ^ 1 for k in first], [k ^ 1 for k in later], later)
    else:
        plans = (list(range(micro)),)
    capacity = max(len(p) for p in plans) * max(per, 1) * ((nblk + 1) // 2) + 3 * GROUP + 2
    oh, tasks = call(
        functools.partial(index_kernel, plans, per if direct else 0, nblk, block, nb),
        (struct((hist_dev, LANES), BF16), pltpu.SMEM((3 * len(plans), capacity), jnp.int32)),
        hist_len, visible, hist_bucket.reshape(-1, LANES),
        smem=(0, 1), smem_out=(1,),
    )
    for layer in range(layers):
        last = layer == layers - 1
        vt = call(
            functools.partial(turn_kernel, layer, nblk, block),
            struct((nblk + 1, width, block), BF16),
            hist_len, value_cache,
            smem=(0,),
        )
        own, gates = call(
            functools.partial(rest_kernel, layer, dh),
            (struct((rows, width), F32),) * 2,
            normed, q, weights,
        )
        if not direct:
            moved = lax.all_gather(q, "hist", axis=0, tiled=True)
            (out,) = attend(layer, [moved], 0, vt, 1)
            moved = lax.all_to_all(out.reshape(n, rows, width), "hist", 0, 0)
            parts = [moved[i] for i in range(n)] + [own]
        else:
            near = {0: q}
            for k in even:
                near[k] = swap(q, k)
            across = {k: swap(near[k], 1) for k in columns}
            if layer == 0:
                w_other, near[0] = lax.optimization_barrier((w_other, near[0]))
            own, gates, near[first[-1]] = lax.optimization_barrier((own, gates, near[first[-1]]))

            def add(ks, outs, back, extra):
                kinds = [F32 if k == 0 else BF16 for k in ks]
                totals = call(
                    functools.partial(add_kernel, len(extra), half),
                    [struct((rows, width), kind) for kind in kinds],
                    *outs, back, *extra,
                )
                return list(totals)

            outs = attend(layer, [near[k] for k in first], 0, vt, half)
            far, outs = lax.optimization_barrier(([across[k] for k in first], outs))
            (far,) = attend(layer, far, 1, vt, 1)
            far_later, far = lax.optimization_barrier(([across[k] for k in later], far))
            back = swap(far, 1)
            (far_later,) = attend(layer, far_later, 2, vt, 1)
            back, far_later = lax.optimization_barrier((back, far_later))
            sums = add(first, outs, back, [])
            pending, sums, far_later = lax.optimization_barrier(([near[k] for k in later], sums, far_later))
            sent = [swap(total, k) for total, k in zip(sums, first)]
            back = swap(far_later, 1)
            outs = attend(layer, pending, 3, vt, half)
            sums = add(later, outs, back, [own])
            parts = [sums[-1]] + sent + [swap(total, k) for total, k in zip(sums, later[:-1])]
        mine = call(combine_kernel, struct((rows, 2 * width), F32), *parts, gates)
        other = swap_heads(mine)
        common = [mine, other, w_out, w_other, stream]
        if last:
            return call(
                functools.partial(finish_kernel, layer, True), struct((rows, d), BF16), *common
            )
        outs = (struct((rows, d), F32), struct((rows, d), BF16), struct((rows, width), BF16))
        stream, normed, q = call(
            functools.partial(finish_kernel, layer, False), outs, *common, weights
        )


def solution(mesh):
    placed = (
        P(("users", "hist"), None),
        P(None, ("users", "hist"), "head"),
        P(None, ("users", "hist"), "head"),
        P(None, None, None, "head"),
        P(None, "head", None),
        P(None, None, "head"),
        P(("users", "hist")),
        P(("users", "hist")),
        P(None, ("users", "hist")),
    )
    return jax.shard_map(
        functools.partial(shards, mesh.shape["hist"]),
        mesh=mesh,
        in_specs=placed,
        out_specs=P(("users", "hist"), None),
        check_vma=False,
    )
```

```python
import functools
import jax
import jax.numpy as jnp
from jax import lax
from jax.experimental import pallas as pl
from jax.experimental.pallas import tpu as pltpu
from jax.sharding import PartitionSpec as P

epsilon = 1e-05
LANES = 128
GROUP = 1
F32, BF16 = jnp.float32, jnp.bfloat16
NT = (((1,), (1,)), ((), ()))
NN = (((1,), (0,)), ((), ()))
SMEM = pl.BlockSpec(memory_space=pltpu.SMEM)
VMEM = pl.BlockSpec(memory_space=pltpu.VMEM)


def half_silu(y):
    return y + y * jnp.tanh(y)


def norm_rows(x):
    mean = jnp.mean(x, axis=-1, keepdims=True)
    centred = x - mean
    variance = jnp.mean(centred * centred, axis=-1, keepdims=True)
    return (centred * lax.rsqrt(variance + epsilon)).astype(BF16)


def mm(a, b, dims=NN):
    return lax.dot_general(a, b, dims, preferred_element_type=F32)


def first_kernel(x_ref, w_ref, normed_ref, q_ref):
    layer = -1
    normed = norm_rows(x_ref[...].astype(F32))
    normed_ref[...] = normed
    q_ref[...] = half_silu(0.5 * mm(normed, w_ref[layer + 1, 0])).astype(BF16)


def rest_kernel(layer, dh, normed_ref, q_ref, w_ref, own_ref, gate_ref):
    normed = normed_ref[...]
    part = lambda j: half_silu(0.5 * mm(normed, w_ref[layer, j])).astype(BF16)
    product = q_ref[...].astype(F32) * part(1).astype(F32)
    head = lax.broadcasted_iota(jnp.int32, product.shape, 1) // dh
    score = jnp.zeros_like(product)
    for h in range(product.shape[1] // dh):
        total = jnp.sum(jnp.where(head == h, product, 0.0), axis=-1, keepdims=True)
        score = jnp.where(head == h, half_silu(total * (0.5 * dh**-0.5)), score)
    own_ref[...] = score * part(2).astype(F32)
    gate_ref[...] = part(3).astype(F32)


def index_kernel(plans, per, nblk, block, nb, len_ref, vis_ref, bucket_ref, oh_ref, task_ref):
    count = len_ref[0]
    me = lax.axis_index("hist")
    for p, ks in enumerate(plans):
        slot_row, first_row, second_row = 3 * p, 3 * p + 1, 3 * p + 2
        total = jnp.int32(0)
        for slot in range(len(ks) * max(per, 1)):
            m = (me ^ ks[slot // per]) * per + slot % per if per else slot
            filled = jnp.int32(0)
            for b in range(nblk):
                place = 1 + total + filled // 2
                task_ref[slot_row, place] = slot
                task_ref[first_row + filled % 2, place] = b
                ok = jnp.logical_and(vis_ref[m, b] != 0, b * block < count)
                filled = filled + jnp.where(ok, 1, 0)
            task_ref[second_row, 1 + total + filled // 2] = nblk
            total = total + (filled + 1) // 2
        task_ref[slot_row, 0] = total
        for place in [1 + total + g for g in range(3 * GROUP)]:
            task_ref[slot_row, place] = len(ks) * max(per, 1)
            task_ref[first_row, place] = nblk
            task_ref[second_row, place] = nblk
    row = lax.broadcasted_iota(jnp.int32, (LANES, LANES), 0)
    for r in range(bucket_ref.shape[0]):
        bucket = jnp.broadcast_to(bucket_ref[r : r + 1, :], (LANES, LANES))
        hit = jnp.logical_and(bucket == row % nb, row < 3 * nb)
        oh_ref[r * LANES : (r + 1) * LANES, :] = jnp.where(hit, 1.0, 0.0).T.astype(BF16)


def turn_kernel(layer, nblk, block, len_ref, v_ref, vt_ref):
    count = len_ref[0]
    width = v_ref.shape[2]
    lane = lax.broadcasted_iota(jnp.int32, (width, block), 1)
    for b in range(nblk):
        turned = v_ref[layer, b * block : (b + 1) * block, :].astype(F32).T
        vt_ref[b] = jnp.where(lane + b * block < count, turned, 0.0).astype(BF16)
    vt_ref[nblk] = jnp.zeros((width, block), BF16)


def attend_kernel(plan, pieces, outs, layer, nblk, block, dh, task_ref, rab_ref, k_ref, oh_ref, vt_ref, *rest):
    q_refs, out_refs = rest[:pieces], rest[pieces : pieces + outs]
    w_ref, acc_ref, *scratch = rest[pieces + outs :]
    units, width, unit = acc_ref.shape[0] - 1, acc_ref.shape[1], acc_ref.shape[2]
    heads = width // dh
    pair_width = 2 * dh
    per = q_refs[0].shape[0] // unit
    nb = rab_ref.shape[2]
    slot_row, first_row, second_row = 3 * plan, 3 * plan + 1, 3 * plan + 2
    table = 0.5 * jnp.concatenate([rab_ref[layer]] * (LANES // nb), axis=1)
    lane = lax.broadcasted_iota(jnp.int32, table.shape, 1)
    high = table.astype(BF16).astype(F32)
    mid = (table - high).astype(BF16).astype(F32)
    low = table - high - mid
    bias = jnp.where(lane < nb, high, jnp.where(lane < 2 * nb, mid, jnp.where(lane < 3 * nb, low, 0.0)))
    qlane = lax.broadcasted_iota(jnp.int32, (unit, pair_width), 1)
    for p in range(pieces):
        for u in range(per):
            slot = p * per + u
            rows = q_refs[p][u * unit : (u + 1) * unit, :].astype(F32) * (0.5 * dh**-0.5)
            for pair in range(heads // 2):
                part = rows[:, pair * pair_width : (pair + 1) * pair_width]
                for h in range(2):
                    mine = jnp.logical_and(qlane >= h * dh, qlane < (h + 1) * dh)
                    span = slice(h * unit, (h + 1) * unit)
                    w_ref[slot, pair, span, 0:pair_width] = jnp.where(mine, part, 0.0).astype(BF16)
                    head = 2 * pair + h
                    w_ref[slot, pair, span, pair_width:] = jnp.broadcast_to(
                        bias[head : head + 1, :], (unit, LANES)
                    ).astype(BF16)

    def score(t, score_ref, pair):
        slot = task_ref[slot_row, 1 + t]
        span = slice(pair * pair_width, (pair + 1) * pair_width)
        keys, hot = [], []
        for row in (first_row, second_row):
            b = task_ref[row, 1 + t]
            start = pl.multiple_of(jnp.where(b == nblk, 0, b) * block, block)
            keys.append(k_ref[layer, pl.ds(start, block), span])
            hot.append(oh_ref[pl.ds(start, block), :])
        left = jnp.concatenate([jnp.concatenate(keys, axis=0), jnp.concatenate(hot, axis=0)], axis=1)
        score_ref[pair] = mm(left, w_ref[slot, pair], NT)

    def gather(t, score_ref, pair):
        first, second = task_ref[first_row, 1 + t], task_ref[second_row, 1 + t]
        weights = half_silu(score_ref[pair]).astype(BF16)
        terms = []
        for h in range(2):
            span = slice((2 * pair + h) * dh, (2 * pair + h + 1) * dh)
            values = jnp.concatenate([vt_ref[first, span, :], vt_ref[second, span, :]], axis=1)
            terms.append(mm(values, weights[:, h * unit : (h + 1) * unit]))
        return terms

    def add(t, terms):
        slot = task_ref[slot_row, 1 + t]
        for head, term in enumerate(terms):
            acc_ref[slot, head * dh : (head + 1) * dh, :] += term

    for slot in range(units):
        acc_ref[slot] = jnp.zeros(acc_ref.shape[1:], F32)
    pairs = range(heads // 2)
    sets = (scratch[:GROUP], scratch[GROUP:])
    for x in range(GROUP):
        for pair in pairs:
            score(x, sets[0][x], pair)

    def group(i, carry):
        for side in range(2):
            now = GROUP * (2 * i + side)
            terms = [[] for _ in range(GROUP)]
            for x in range(GROUP):
                for pair in pairs:
                    score(now + GROUP + x, sets[1 - side][x], pair)
                    terms[x] += gather(now + x, sets[side][x], pair)
            for x in range(GROUP):
                add(now + x, terms[x])
        return carry

    lax.fori_loop(0, (task_ref[slot_row, 0] + 2 * GROUP - 1) // (2 * GROUP), group, 0)
    share = units // outs
    for slot in range(units):
        place = slot % share * unit
        out_refs[slot // share][place : place + unit, :] = acc_ref[slot].T.astype(BF16)


def combine_kernel(*refs):
    *parts, gate_ref, out_ref = refs
    total = sum(part[...].astype(F32) for part in parts)
    width = total.shape[1]
    out_ref[:, :width] = total
    out_ref[:, width:] = gate_ref[...]


def finish_kernel(layer, last, mine_ref, other_ref, wa_ref, wb_ref, stream_ref, *rest):
    lead = lax.axis_index("head") == 0
    width = mine_ref.shape[1] // 2
    mine, other = mine_ref[...], other_ref[...]
    first, second = jnp.where(lead, mine, other), jnp.where(lead, other, mine)
    att = [first[:, :width], second[:, :width]]
    gates = [first[:, width:], second[:, width:]]
    total = sum(jnp.sum(a, axis=-1, keepdims=True) for a in att) / (2 * width)
    square = sum(jnp.sum(a * a, axis=-1, keepdims=True) for a in att) / (2 * width)
    scale = lax.rsqrt(square - total * total + epsilon)
    gated = [((a - total) * scale * g).astype(BF16) for a, g in zip(att, gates)]
    wa, wb = wa_ref[layer], wb_ref[layer]
    update = mm(gated[0], jnp.where(lead, wa, wb)) + mm(gated[1], jnp.where(lead, wb, wa))
    stream = stream_ref[...].astype(F32) + update
    if last:
        (out_ref,) = rest
        out_ref[...] = stream.astype(BF16)
        return
    w_ref, out_ref, normed_ref, q_ref = rest
    out_ref[...] = stream
    normed = norm_rows(stream)
    normed_ref[...] = normed
    q_ref[...] = half_silu(0.5 * mm(normed, w_ref[layer + 1, 0])).astype(BF16)


def add_kernel(owns, pieces, *refs):
    outs, moved = refs[:pieces], refs[pieces]
    results = refs[pieces + 1 + owns :]
    rows = outs[0].shape[0]
    for p in range(pieces):
        total = outs[p][...].astype(F32) + moved[p * rows : (p + 1) * rows, :].astype(F32)
        if owns and p == pieces - 1:
            results[p][...] = total + refs[pieces + 1][...]
        else:
            results[p][...] = total.astype(BF16)


def struct(shape, kind):
    return jax.ShapeDtypeStruct(shape, kind)


def call(kernel, out_shape, *args, smem=(), smem_out=(), scratch=(), vmem=8, flops=10**7):
    outs = out_shape if isinstance(out_shape, (list, tuple)) else [out_shape]
    specs = [SMEM if i in smem_out else VMEM for i in range(len(outs))]
    size = sum(a.size * a.dtype.itemsize for a in args) + 4 * len(outs)
    return pl.pallas_call(
        kernel,
        out_shape=out_shape,
        in_specs=[SMEM if i in smem else VMEM for i in range(len(args))],
        out_specs=specs if isinstance(out_shape, (list, tuple)) else specs[0],
        scratch_shapes=list(scratch),
        compiler_params=pltpu.CompilerParams(vmem_limit_bytes=vmem << 20),
        cost_estimate=pl.CostEstimate(flops=flops, bytes_accessed=size, transcendentals=0),
    )(*args)


def shards(n, candidates, key_cache, value_cache, w_in, w_out, rab_table, hist_len, hist_bucket, visible):
    layers, hist_dev, width = key_cache.shape
    heads = rab_table.shape[2]
    nb = rab_table.shape[1]
    dh = width // heads
    micro, nblk = visible.shape
    block = hist_dev // nblk
    rows, d = candidates.shape
    unit = rows * n // micro
    per = rows // unit
    direct = per > 0 and n >= 4 and n & (n - 1) == 0
    even = list(range(2, n, 2))[::-1]

    def attend(layer, pieces, plan, vt, outs):
        units = sum(p.shape[0] for p in pieces) // unit
        return call(
            functools.partial(attend_kernel, plan, len(pieces), outs, layer, nblk, block, dh),
            [struct((units * unit // outs, width), BF16)] * outs,
            pltpu.with_memory_space_constraint(tasks, pltpu.SMEM), table, key_cache, oh, vt, *pieces,
            smem=(0,),
            scratch=[
                pltpu.VMEM((units + 1, heads // 2, 2 * unit, 2 * LANES), BF16),
                pltpu.VMEM((units + 1, width, unit), F32),
            ]
            + [pltpu.VMEM((heads // 2, 2 * block, 2 * unit), kind) for kind in [F32] * (2 * GROUP)],
            vmem=16,
            flops=units * unit * hist_dev * width * 8,
        )

    def swap(x, k):
        return lax.ppermute(x, "hist", [(i, i ^ k) for i in range(n)])

    swap_heads = lambda x: lax.ppermute(x, "head", [(0, 1), (1, 0)])
    weights = w_in.transpose(0, 2, 1, 3)
    table = rab_table.transpose(0, 2, 1)
    normed, q = call(
        first_kernel,
        (struct((rows, d), BF16), struct((rows, width), BF16)),
        candidates, weights,
    )
    stream = candidates
    if direct:
        columns = even + [0]
        half = n // 4
        first, later = columns[:half], columns[half:]
        plans = (first, [k ^ 1 for k in first], [k ^ 1 for k in later], later)
    else:
        plans = (list(range(micro)),)
    capacity = max(len(p) for p in plans) * max(per, 1) * ((nblk + 1) // 2) + 3 * GROUP + 2
    oh, tasks = call(
        functools.partial(index_kernel, plans, per if direct else 0, nblk, block, nb),
        (struct((hist_dev, LANES), BF16), pltpu.SMEM((3 * len(plans), capacity), jnp.int32)),
        hist_len, visible, hist_bucket.reshape(-1, LANES),
        smem=(0, 1), smem_out=(1,),
    )
    for layer in range(layers):
        last = layer == layers - 1
        vt = call(
            functools.partial(turn_kernel, layer, nblk, block),
            struct((nblk + 1, width, block), BF16),
            hist_len, value_cache,
            smem=(0,),
        )
        own, gates = call(
            functools.partial(rest_kernel, layer, dh),
            (struct((rows, width), F32),) * 2,
            normed, q, weights,
        )
        if not direct:
            w_other = swap_heads(w_out)
            moved = lax.all_gather(q, "hist", axis=0, tiled=True)
            (out,) = attend(layer, [moved], 0, vt, 1)
            moved = lax.all_to_all(out.reshape(n, rows, width), "hist", 0, 0)
            parts = [moved[i] for i in range(n)] + [own]
        else:
            near = {0: q}
            for k in even:
                near[k] = swap(q, k)
            across = {k: swap(near[k], 1) for k in columns}
            if layer == 0:
                lead, source = lax.optimization_barrier((near[columns[-2]], w_out))
                near[columns[-2]] = lead
                w_other = swap_heads(source)
            own, gates, near[first[-1]] = lax.optimization_barrier((own, gates, near[first[-1]]))

            def add(ks, outs, back, extra):
                kinds = [F32 if k == 0 else BF16 for k in ks]
                totals = call(
                    functools.partial(add_kernel, len(extra), half),
                    [struct((rows, width), kind) for kind in kinds],
                    *outs, back, *extra,
                )
                return list(totals)

            outs = attend(layer, [near[k] for k in first], 0, vt, half)
            far, outs = lax.optimization_barrier(([across[k] for k in first], outs))
            (far,) = attend(layer, far, 1, vt, 1)
            far_later, far = lax.optimization_barrier(([across[k] for k in later], far))
            back = swap(far, 1)
            (far_later,) = attend(layer, far_later, 2, vt, 1)
            back, far_later = lax.optimization_barrier((back, far_later))
            sums = add(first, outs, back, [])
            pending, sums, far_later = lax.optimization_barrier(([near[k] for k in later], sums, far_later))
            sent = [swap(total, k) for total, k in zip(sums, first)]
            back = swap(far_later, 1)
            outs = attend(layer, pending, 3, vt, half)
            sums = add(later, outs, back, [own])
            parts = [sums[-1]] + sent + [swap(total, k) for total, k in zip(sums, later[:-1])]
        mine = call(combine_kernel, struct((rows, 2 * width), F32), *parts, gates)
        other = swap_heads(mine)
        common = [mine, other, w_out, w_other, stream]
        if last:
            return call(
                functools.partial(finish_kernel, layer, True), struct((rows, d), BF16), *common
            )
        outs = (struct((rows, d), F32), struct((rows, d), BF16), struct((rows, width), BF16))
        stream, normed, q = call(
            functools.partial(finish_kernel, layer, False), outs, *common, weights
        )


def solution(mesh):
    placed = (
        P(("users", "hist"), None),
        P(None, ("users", "hist"), "head"),
        P(None, ("users", "hist"), "head"),
        P(None, None, None, "head"),
        P(None, "head", None),
        P(None, None, "head"),
        P(("users", "hist")),
        P(("users", "hist")),
        P(None, ("users", "hist")),
    )
    return jax.shard_map(
        functools.partial(shards, mesh.shape["hist"]),
        mesh=mesh,
        in_specs=placed,
        out_specs=P(("users", "hist"), None),
        check_vma=False,
    )
```

```python
import functools
import jax
import jax.numpy as jnp
from jax import lax
from jax.experimental import pallas as pl
from jax.experimental.pallas import tpu as pltpu
from jax.sharding import PartitionSpec as P

epsilon = 1e-05
LANES = 128
GROUP = 1
F32, BF16 = jnp.float32, jnp.bfloat16
NT = (((1,), (1,)), ((), ()))
NN = (((1,), (0,)), ((), ()))
SMEM = pl.BlockSpec(memory_space=pltpu.SMEM)
VMEM = pl.BlockSpec(memory_space=pltpu.VMEM)


def half_silu(y):
    return y + y * jnp.tanh(y)


def norm_rows(x):
    mean = jnp.mean(x, axis=-1, keepdims=True)
    centred = x - mean
    variance = jnp.mean(centred * centred, axis=-1, keepdims=True)
    return (centred * lax.rsqrt(variance + epsilon)).astype(BF16)


def mm(a, b, dims=NN):
    return lax.dot_general(a, b, dims, preferred_element_type=F32)


def first_kernel(x_ref, w_ref, normed_ref, q_ref):
    layer = -1
    normed = norm_rows(x_ref[...].astype(F32))
    normed_ref[...] = normed
    q_ref[...] = half_silu(0.5 * mm(normed, w_ref[layer + 1, 0])).astype(BF16)


def rest_kernel(layer, dh, normed_ref, q_ref, w_ref, own_ref, gate_ref):
    normed = normed_ref[...]
    part = lambda j: half_silu(0.5 * mm(normed, w_ref[layer, j])).astype(BF16)
    product = q_ref[...].astype(F32) * part(1).astype(F32)
    head = lax.broadcasted_iota(jnp.int32, product.shape, 1) // dh
    score = jnp.zeros_like(product)
    for h in range(product.shape[1] // dh):
        total = jnp.sum(jnp.where(head == h, product, 0.0), axis=-1, keepdims=True)
        score = jnp.where(head == h, half_silu(total * (0.5 * dh**-0.5)), score)
    own_ref[...] = score * part(2).astype(F32)
    gate_ref[...] = part(3).astype(F32)


def index_kernel(plans, per, nblk, block, nb, len_ref, vis_ref, bucket_ref, oh_ref, task_ref):
    count = len_ref[0]
    me = lax.axis_index("hist")
    for p, ks in enumerate(plans):
        slot_row, first_row, second_row = 3 * p, 3 * p + 1, 3 * p + 2
        total = jnp.int32(0)
        for slot in range(len(ks) * max(per, 1)):
            m = (me ^ ks[slot // per]) * per + slot % per if per else slot
            filled = jnp.int32(0)
            for b in range(nblk):
                place = 1 + total + filled // 2
                task_ref[slot_row, place] = slot
                task_ref[first_row + filled % 2, place] = b
                ok = jnp.logical_and(vis_ref[m, b] != 0, b * block < count)
                filled = filled + jnp.where(ok, 1, 0)
            task_ref[second_row, 1 + total + filled // 2] = nblk
            total = total + (filled + 1) // 2
        task_ref[slot_row, 0] = total
        for place in [1 + total + g for g in range(3 * GROUP)]:
            task_ref[slot_row, place] = len(ks) * max(per, 1)
            task_ref[first_row, place] = nblk
            task_ref[second_row, place] = nblk
    row = lax.broadcasted_iota(jnp.int32, (LANES, LANES), 0)
    for r in range(bucket_ref.shape[0]):
        bucket = jnp.broadcast_to(bucket_ref[r : r + 1, :], (LANES, LANES))
        hit = jnp.logical_and(bucket == row % nb, row < 3 * nb)
        oh_ref[r * LANES : (r + 1) * LANES, :] = jnp.where(hit, 1.0, 0.0).astype(BF16).T


def turn_kernel(layer, nblk, block, len_ref, v_ref, vt_ref):
    count = len_ref[0]
    width = v_ref.shape[2]
    lane = lax.broadcasted_iota(jnp.int32, (width, block), 1)
    for b in range(nblk):
        turned = v_ref[layer, b * block : (b + 1) * block, :].T.astype(F32)
        vt_ref[b] = jnp.where(lane + b * block < count, turned, 0.0).astype(BF16)
    vt_ref[nblk] = jnp.zeros((width, block), BF16)


def attend_kernel(plan, pieces, outs, layer, nblk, block, dh, task_ref, rab_ref, k_ref, oh_ref, vt_ref, *rest):
    q_refs, out_refs = rest[:pieces], rest[pieces : pieces + outs]
    w_ref, acc_ref, *scratch = rest[pieces + outs :]
    units, width, unit = acc_ref.shape[0] - 1, acc_ref.shape[1], acc_ref.shape[2]
    heads = width // dh
    pair_width = 2 * dh
    per = q_refs[0].shape[0] // unit
    nb = rab_ref.shape[2]
    slot_row, first_row, second_row = 3 * plan, 3 * plan + 1, 3 * plan + 2
    table = 0.5 * jnp.concatenate([rab_ref[layer]] * (LANES // nb), axis=1)
    lane = lax.broadcasted_iota(jnp.int32, table.shape, 1)
    high = table.astype(BF16).astype(F32)
    mid = (table - high).astype(BF16).astype(F32)
    low = table - high - mid
    bias = jnp.where(lane < nb, high, jnp.where(lane < 2 * nb, mid, jnp.where(lane < 3 * nb, low, 0.0)))
    qlane = lax.broadcasted_iota(jnp.int32, (unit, pair_width), 1)
    for p in range(pieces):
        for u in range(per):
            slot = p * per + u
            rows = q_refs[p][u * unit : (u + 1) * unit, :].astype(F32) * (0.5 * dh**-0.5)
            for pair in range(heads // 2):
                part = rows[:, pair * pair_width : (pair + 1) * pair_width]
                for h in range(2):
                    mine = jnp.logical_and(qlane >= h * dh, qlane < (h + 1) * dh)
                    span = slice(h * unit, (h + 1) * unit)
                    w_ref[slot, pair, span, 0:pair_width] = jnp.where(mine, part, 0.0).astype(BF16)
                    head = 2 * pair + h
                    w_ref[slot, pair, span, pair_width:] = jnp.broadcast_to(
                        bias[head : head + 1, :], (unit, LANES)
                    ).astype(BF16)

    def score(t, score_ref, pair):
        slot = task_ref[slot_row, 1 + t]
        span = slice(pair * pair_width, (pair + 1) * pair_width)
        keys, hot = [], []
        for row in (first_row, second_row):
            b = task_ref[row, 1 + t]
            start = pl.multiple_of(jnp.where(b == nblk, 0, b) * block, block)
            keys.append(k_ref[layer, pl.ds(start, block), span])
            hot.append(oh_ref[pl.ds(start, block), :])
        left = jnp.concatenate([jnp.concatenate(keys, axis=0), jnp.concatenate(hot, axis=0)], axis=1)
        score_ref[pair] = mm(left, w_ref[slot, pair], NT)

    def gather(t, score_ref, pair):
        first, second = task_ref[first_row, 1 + t], task_ref[second_row, 1 + t]
        weights = half_silu(score_ref[pair]).astype(BF16)
        terms = []
        for h in range(2):
            span = slice((2 * pair + h) * dh, (2 * pair + h + 1) * dh)
            values = jnp.concatenate([vt_ref[first, span, :], vt_ref[second, span, :]], axis=1)
            terms.append(mm(values, weights[:, h * unit : (h + 1) * unit]))
        return terms

    def add(t, terms):
        slot = task_ref[slot_row, 1 + t]
        for head, term in enumerate(terms):
            acc_ref[slot, head * dh : (head + 1) * dh, :] += term

    for slot in range(units):
        acc_ref[slot] = jnp.zeros(acc_ref.shape[1:], F32)
    pairs = range(heads // 2)
    sets = (scratch[:GROUP], scratch[GROUP:])
    for x in range(GROUP):
        for pair in pairs:
            score(x, sets[0][x], pair)

    def group(i, carry):
        for side in range(2):
            now = GROUP * (2 * i + side)
            terms = [[] for _ in range(GROUP)]
            for x in range(GROUP):
                for pair in pairs:
                    score(now + GROUP + x, sets[1 - side][x], pair)
                    terms[x] += gather(now + x, sets[side][x], pair)
            for x in range(GROUP):
                add(now + x, terms[x])
        return carry

    lax.fori_loop(0, (task_ref[slot_row, 0] + 2 * GROUP - 1) // (2 * GROUP), group, 0)
    share = units // outs
    for slot in range(units):
        place = slot % share * unit
        out_refs[slot // share][place : place + unit, :] = acc_ref[slot].T.astype(BF16)


def combine_kernel(*refs):
    *parts, gate_ref, out_ref = refs
    total = sum(part[...].astype(F32) for part in parts)
    width = total.shape[1]
    out_ref[:, :width] = total
    out_ref[:, width:] = gate_ref[...]


def finish_kernel(layer, last, mine_ref, other_ref, wa_ref, wb_ref, stream_ref, *rest):
    lead = lax.axis_index("head") == 0
    width = mine_ref.shape[1] // 2
    mine, other = mine_ref[...], other_ref[...]
    first, second = jnp.where(lead, mine, other), jnp.where(lead, other, mine)
    att = [first[:, :width], second[:, :width]]
    gates = [first[:, width:], second[:, width:]]
    total = sum(jnp.sum(a, axis=-1, keepdims=True) for a in att) / (2 * width)
    square = sum(jnp.sum(a * a, axis=-1, keepdims=True) for a in att) / (2 * width)
    scale = lax.rsqrt(square - total * total + epsilon)
    gated = [((a - total) * scale * g).astype(BF16) for a, g in zip(att, gates)]
    wa, wb = wa_ref[layer], wb_ref[layer]
    update = mm(gated[0], jnp.where(lead, wa, wb)) + mm(gated[1], jnp.where(lead, wb, wa))
    stream = stream_ref[...].astype(F32) + update
    if last:
        (out_ref,) = rest
        out_ref[...] = stream.astype(BF16)
        return
    w_ref, out_ref, normed_ref, q_ref = rest
    out_ref[...] = stream
    normed = norm_rows(stream)
    normed_ref[...] = normed
    q_ref[...] = half_silu(0.5 * mm(normed, w_ref[layer + 1, 0])).astype(BF16)


def add_kernel(owns, pieces, *refs):
    outs, moved = refs[:pieces], refs[pieces]
    results = refs[pieces + 1 + owns :]
    rows = outs[0].shape[0]
    for p in range(pieces):
        total = outs[p][...].astype(F32) + moved[p * rows : (p + 1) * rows, :].astype(F32)
        if owns and p == pieces - 1:
            results[p][...] = total + refs[pieces + 1][...]
        else:
            results[p][...] = total.astype(BF16)


def struct(shape, kind):
    return jax.ShapeDtypeStruct(shape, kind)


def call(kernel, out_shape, *args, smem=(), smem_out=(), scratch=(), vmem=8, flops=10**7):
    outs = out_shape if isinstance(out_shape, (list, tuple)) else [out_shape]
    specs = [SMEM if i in smem_out else VMEM for i in range(len(outs))]
    size = sum(a.size * a.dtype.itemsize for a in args) + 4 * len(outs)
    return pl.pallas_call(
        kernel,
        out_shape=out_shape,
        in_specs=[SMEM if i in smem else VMEM for i in range(len(args))],
        out_specs=specs if isinstance(out_shape, (list, tuple)) else specs[0],
        scratch_shapes=list(scratch),
        compiler_params=pltpu.CompilerParams(vmem_limit_bytes=vmem << 20),
        cost_estimate=pl.CostEstimate(flops=flops, bytes_accessed=size, transcendentals=0),
    )(*args)


def shards(n, candidates, key_cache, value_cache, w_in, w_out, rab_table, hist_len, hist_bucket, visible):
    layers, hist_dev, width = key_cache.shape
    heads = rab_table.shape[2]
    nb = rab_table.shape[1]
    dh = width // heads
    micro, nblk = visible.shape
    block = hist_dev // nblk
    rows, d = candidates.shape
    unit = rows * n // micro
    per = rows // unit
    direct = per > 0 and n >= 4 and n & (n - 1) == 0
    even = list(range(2, n, 2))[::-1]

    def attend(layer, pieces, plan, vt, outs):
        units = sum(p.shape[0] for p in pieces) // unit
        return call(
            functools.partial(attend_kernel, plan, len(pieces), outs, layer, nblk, block, dh),
            [struct((units * unit // outs, width), BF16)] * outs,
            pltpu.with_memory_space_constraint(tasks, pltpu.SMEM), table, key_cache, oh, vt, *pieces,
            smem=(0,),
            scratch=[
                pltpu.VMEM((units + 1, heads // 2, 2 * unit, 2 * LANES), BF16),
                pltpu.VMEM((units + 1, width, unit), F32),
            ]
            + [pltpu.VMEM((heads // 2, 2 * block, 2 * unit), kind) for kind in [F32] * (2 * GROUP)],
            vmem=16,
            flops=units * unit * hist_dev * width * 8,
        )

    def swap(x, k):
        return lax.ppermute(x, "hist", [(i, i ^ k) for i in range(n)])

    swap_heads = lambda x: lax.ppermute(x, "head", [(0, 1), (1, 0)])
    weights = w_in.transpose(0, 2, 1, 3)
    table = rab_table.transpose(0, 2, 1)
    normed, q = call(
        first_kernel,
        (struct((rows, d), BF16), struct((rows, width), BF16)),
        candidates, weights,
    )
    stream = candidates
    w_other = swap_heads(w_out)
    if direct:
        columns = even + [0]
        half = n // 4
        first, later = columns[:half], columns[half:]
        plans = (first, [k ^ 1 for k in first], [k ^ 1 for k in later], later)
    else:
        plans = (list(range(micro)),)
    capacity = max(len(p) for p in plans) * max(per, 1) * ((nblk + 1) // 2) + 3 * GROUP + 2
    oh, tasks = call(
        functools.partial(index_kernel, plans, per if direct else 0, nblk, block, nb),
        (struct((hist_dev, LANES), BF16), pltpu.SMEM((3 * len(plans), capacity), jnp.int32)),
        hist_len, visible, hist_bucket.reshape(-1, LANES),
        smem=(0, 1), smem_out=(1,),
    )
    for layer in range(layers):
        last = layer == layers - 1
        vt = call(
            functools.partial(turn_kernel, layer, nblk, block),
            struct((nblk + 1, width, block), BF16),
            hist_len, value_cache,
            smem=(0,),
        )
        own, gates = call(
            functools.partial(rest_kernel, layer, dh),
            (struct((rows, width), F32),) * 2,
            normed, q, weights,
        )
        if not direct:
            moved = lax.all_gather(q, "hist", axis=0, tiled=True)
            (out,) = attend(layer, [moved], 0, vt, 1)
            moved = lax.all_to_all(out.reshape(n, rows, width), "hist", 0, 0)
            parts = [moved[i] for i in range(n)] + [own]
        else:
            near = {0: q}
            for k in even:
                near[k] = swap(q, k)
            across = {k: swap(near[k], 1) for k in columns}
            if layer == 0:
                w_other, near[0] = lax.optimization_barrier((w_other, near[0]))
            own, gates, near[first[-1]] = lax.optimization_barrier((own, gates, near[first[-1]]))

            def add(ks, outs, back, extra):
                kinds = [F32 if k == 0 else BF16 for k in ks]
                totals = call(
                    functools.partial(add_kernel, len(extra), half),
                    [struct((rows, width), kind) for kind in kinds],
                    *outs, back, *extra,
                )
                return list(totals)

            outs = attend(layer, [near[k] for k in first], 0, vt, half)
            far, outs = lax.optimization_barrier(([across[k] for k in first], outs))
            (far,) = attend(layer, far, 1, vt, 1)
            far_later, far = lax.optimization_barrier(([across[k] for k in later], far))
            back = swap(far, 1)
            (far_later,) = attend(layer, far_later, 2, vt, 1)
            back, far_later = lax.optimization_barrier((back, far_later))
            sums = add(first, outs, back, [])
            pending, sums, far_later = lax.optimization_barrier(([near[k] for k in later], sums, far_later))
            sent = [swap(total, k) for total, k in zip(sums, first)]
            back = swap(far_later, 1)
            outs = attend(layer, pending, 3, vt, half)
            sums = add(later, outs, back, [own])
            parts = [sums[-1]] + sent + [swap(total, k) for total, k in zip(sums, later[:-1])]
        mine = call(combine_kernel, struct((rows, 2 * width), F32), *parts, gates)
        other = swap_heads(mine)
        common = [mine, other, w_out, w_other, stream]
        if last:
            return call(
                functools.partial(finish_kernel, layer, True), struct((rows, d), BF16), *common
            )
        outs = (struct((rows, d), F32), struct((rows, d), BF16), struct((rows, width), BF16))
        stream, normed, q = call(
            functools.partial(finish_kernel, layer, False), outs, *common, weights
        )


def solution(mesh):
    placed = (
        P(("users", "hist"), None),
        P(None, ("users", "hist"), "head"),
        P(None, ("users", "hist"), "head"),
        P(None, None, None, "head"),
        P(None, "head", None),
        P(None, None, "head"),
        P(("users", "hist")),
        P(("users", "hist")),
        P(None, ("users", "hist")),
    )
    return jax.shard_map(
        functools.partial(shards, mesh.shape["hist"]),
        mesh=mesh,
        in_specs=placed,
        out_specs=P(("users", "hist"), None),
        check_vma=False,
    )
```
